128 devices in a mesh: rows: 16 (over z, x), cents: 8 (over y, core).
Axes of the slice: x: 4, y: 4, z: 4, core: 2. Of those that a mesh axis runs over, the one named last changes fastest.
Arguments:
- groups: bfloat16 [262144, 1024], P(('rows', 'cents')), may hold values from -60 to 60
- centroids: bfloat16 [262144, 1024], P(('rows', 'cents')), may hold values from -60 to 60
- row_weight: float32 [262144], P(('rows', 'cents')), may hold values from 0.5 to 18
- block_ids: int32 [1024, 8], P(('rows', 'cents')), may hold values from 0 to 2047, as said below
- block_counts: int32 [1024], P(('rows', 'cents')), may hold values from 1 to 8
Outputs:
- centroid_sums: float32 [262144, 1024], P(('rows', 'cents'))
- column_load: float32 [262144], P(('rows', 'cents'))
The draws below stay inside these ranges and needn't reach their ends.
Inputs may be any that keep to these rules, and one draw needn't show every extreme that they name: `block_ids`: slots k < block_counts[b] are the candidates of row block b; later slots hold valid ids but are unused. List block g is held by the device of index g // 16 in the order rows, then cents. The 8 x 8 slots of the row blocks held by device (r, c) name blocks held by devices (o, c) only, exactly 4 slots for each o, and among those slots exactly 2 distinct blocks of o; the slots of one row block name blocks of distinct holders.
All inputs are finite; a program needn't handle non-finite values.
Results may differ from the reference program's by a relative error of at most 0.0051.
Values may be sent and summed in bfloat16 or wider, within the bound.
No kernel may reach another device: no remote copies, remote signals or barrier semaphores. Data moves between devices by JAX's collectives and lax.ppermute only.
A program may use at most 192 MiB of HBM per device.

```python
import math
import jax
import jax.numpy as jnp
from jax import lax

D = 1024
RB = 256
CB = 128
MAXC = 8
USE = 2
ITERS = 3
NBD = 8
CBD = 16
ROWS = 262144
NBLK = 1024
K = 262144
N_ROWS = 16
N_CENTS = 8
DEVICES = 128


def scaled_vectors(key, count):
    first, second, third = jax.random.split(key, 3)
    row_factor = jnp.exp(jax.random.uniform(first, (count, 1), jnp.float32, 0.0, math.log(10.0)))
    column_factor = jnp.exp(jax.random.uniform(second, (1, D), jnp.float32, 0.0, math.log(10.0)))
    noise = jnp.clip(jax.random.normal(third, (count, D), jnp.float32), -5.0, 5.0)
    return row_factor * column_factor * noise * 0.1


def draw_groups(key, part):
    return scaled_vectors(jax.random.fold_in(key, 11), ROWS).astype(jnp.bfloat16)


def draw_centroids(key, part):
    return scaled_vectors(jax.random.fold_in(key, 13), K).astype(jnp.bfloat16)


def draw_row_weight(key, part):
    position = jnp.arange(ROWS, dtype=jnp.float32) / (ROWS - 1)
    inner_key = jax.random.fold_in(key, 23)
    base_values = jnp.exp(jax.random.uniform(inner_key, (ROWS,), jnp.float32, math.log(0.5), math.log(2.0)))
    return base_values * (1.0 + 2.0 * position)


def draw_block_ids(key, part):
    device = jnp.arange(DEVICES, dtype=jnp.int32)
    cents_index = device % N_CENTS
    key_list = jax.random.split(jax.random.fold_in(key, 17), DEVICES)

    def holder_order(single_key):
        return jax.random.permutation(single_key, N_ROWS)
    holder_perm = jax.vmap(holder_order)(key_list).astype(jnp.int32)
    choice_keys = jax.random.split(jax.random.fold_in(key, 19), DEVICES * N_ROWS)

    def block_order(single_key):
        return jax.random.permutation(single_key, CBD)[:USE]
    chosen_blocks = jax.vmap(block_order)(choice_keys).astype(jnp.int32).reshape(DEVICES, N_ROWS, USE)
    slot_index = jnp.arange(NBD * MAXC, dtype=jnp.int32)
    holder_row = holder_perm[:, slot_index % N_ROWS]
    reuse_index = slot_index // N_ROWS % USE
    local_block = chosen_blocks[device[:, None], holder_row, reuse_index[None, :]]
    block_list = (holder_row * N_CENTS + cents_index[:, None]) * CBD + local_block
    return block_list.reshape(NBLK, MAXC).astype(jnp.int32)


def plant(drawn, key, smallest, high):
    longest = drawn.shape.index(max(drawn.shape))
    spots = []
    for shift in (0, 1):
        where = [jax.random.randint(jax.random.fold_in(key, axis), (), 0, length) for axis, length in enumerate(drawn.shape)]
        where[longest] = (where[longest] + shift) % drawn.shape[longest]
        spots.append(tuple(where))
    return drawn.at[spots[0]].set(smallest).at[spots[1]].set(high)


def setup_inputs(seed: int = 0) -> dict:
    key_of = jax.random.split(jax.random.key(seed), 6)
    groups = draw_groups(jax.random.fold_in(key_of[5], 71), 0)
    centroids = draw_centroids(jax.random.fold_in(key_of[5], 71), 0)
    row_weight = draw_row_weight(jax.random.fold_in(key_of[5], 71), 0)
    block_ids = draw_block_ids(jax.random.fold_in(key_of[5], 71), 0)
    block_counts = plant(jax.random.randint(key_of[4], (NBLK,), 1, MAXC + 1), jax.random.fold_in(key_of[4], 1), 1, MAXC).astype(jnp.int32)
    return {"groups": groups, "centroids": centroids, "row_weight": row_weight, "block_ids": block_ids, "block_counts": block_counts}


BETA = 32.0
EPSILON = 1e-06
PRIOR = 0.25
HIGHEST = lax.Precision.HIGHEST

def normalize(values):
    widened = values.astype(jnp.float32)
    factor = lax.rsqrt(lax.optimization_barrier(jnp.mean(widened * widened, axis=-1, keepdims=True)) + EPSILON)
    return (widened * factor).astype(jnp.bfloat16)

def reference(groups, centroids, row_weight, block_ids, block_counts):
    blocks_all = block_ids.shape[0]
    lists_blocks = centroids.shape[0] // CB
    rows_norm = normalize(groups).reshape(blocks_all, RB, D)
    lists_norm = normalize(centroids).reshape(lists_blocks, CB, D)
    live_mask = (jnp.arange(MAXC, dtype=jnp.int32)[None, :] < block_counts[:, None]).astype(jnp.float32)

    def kernel_block(operands):
        row_block, block_row, mask_row = operands
        picked_lists = lists_norm[block_row]
        scores = jnp.einsum('rd,kcd->krc', row_block.astype(jnp.float32), picked_lists.astype(jnp.float32))
        return jnp.exp(scores * (BETA / D)) * mask_row[:, None, None]
    kernel = lax.map(kernel_block, (rows_norm, block_ids, live_mask))
    weights = row_weight.reshape(blocks_all, RB)
    target = jnp.sum(row_weight) / (lists_blocks * CB)
    flat_ids = block_ids.reshape(-1)
    scales = jnp.ones((lists_blocks, CB), jnp.float32)

    def row_pass(scales):
        picked = scales[block_ids]
        row_sums = jnp.einsum('bkrc,bkc->br', kernel, picked, precision=HIGHEST)
        return (weights / row_sums, picked)
    for iteration in range(ITERS):
        row_scale, picked = row_pass(scales)
        column_parts = jnp.einsum('bkrc,br->bkc', kernel, row_scale, precision=HIGHEST)
        column = jax.ops.segment_sum(column_parts.reshape(-1, CB), flat_ids, num_segments=lists_blocks)
        scales = target / (column + PRIOR * target)
    row_scale, picked = row_pass(scales)
    transport = row_scale[:, None, :, None] * kernel * picked[:, :, None, :]
    column_mass = jax.ops.segment_sum(lax.optimization_barrier(jnp.sum(transport, axis=2)).reshape(-1, CB), flat_ids, num_segments=lists_blocks)
    transport_half = transport.astype(jnp.bfloat16)

    def accumulate(totals, operands):
        weight_block, row_block, block_row = operands
        list_parts = jnp.einsum('krc,rd->kcd', weight_block.astype(jnp.float32), row_block.astype(jnp.float32))
        return (totals.at[block_row].add(list_parts), None)
    totals, unused = lax.scan(accumulate, jnp.zeros((lists_blocks, CB, D), jnp.float32), (transport_half, rows_norm, block_ids))
    return (totals.reshape(lists_blocks * CB, D), column_mass.reshape(-1) / target)
```

```python
import jax
import jax.numpy as jnp
from jax import lax
from jax.experimental import pallas as pl
from jax.experimental.pallas import tpu as pltpu
from jax.sharding import PartitionSpec as P

D = 1024
RB = 256
CB = 128
MAXC = 8
USE = 2
ITERS = 3
NBD = 8
CBD = 16
NR = 16
NC = 8
ND = NR * USE
NDX = ND + 8
K_TOTAL = NR * NC * CBD * CB
ROWS_X = USE * CB * (D // 128)
ROWS_P = ROWS_X + 16

BETA = 32.0
EPSILON = 1e-06
PRIOR = 0.25
F32 = jnp.float32
BF16 = jnp.bfloat16


def unit_rows(values):
    widened = values.astype(F32)
    mean = jnp.sum(widened * widened, axis=-1, keepdims=True) * (1.0 / D)
    return (widened * lax.rsqrt(mean + EPSILON)).astype(BF16)


def rows_kernel(groups_ref, out_ref):
    out_ref[...] = unit_rows(groups_ref[...])


def normalize_rows(groups):
    step = 512
    return pl.pallas_call(
        rows_kernel,
        grid=(groups.shape[0] // step,),
        in_specs=[pl.BlockSpec((step, D), lambda i: (i, 0))],
        out_specs=pl.BlockSpec((step, D), lambda i: (i, 0)),
        out_shape=jax.ShapeDtypeStruct(groups.shape, BF16),
        name="rows_norm",
    )(groups)


def pick_kernel(wanted_ref, *refs):
    out_ref = refs[-1]
    for n, block in enumerate(refs[:-1]):
        out_ref[n] = unit_rows(block[0])


def pick_lists(centroids, wanted):
    per = 4
    specs = [
        pl.BlockSpec((1, CB, D), lambda i, w, n=n: (w[i * per + n], 0, 0)) for n in range(per)
    ]
    return pl.pallas_call(
        pick_kernel,
        grid_spec=pltpu.PrefetchScalarGridSpec(
            num_scalar_prefetch=1,
            grid=(ND // per,),
            in_specs=specs,
            out_specs=pl.BlockSpec((per, CB, D), lambda i, w: (i, 0, 0)),
        ),
        out_shape=jax.ShapeDtypeStruct((ND, CB, D), BF16),
        name="pick_lists",
    )(wanted, *([centroids] * per))


def column_pass(kernel_ref, row_scale, dist_ref, b, parts_ref):
    for k in range(MAXC):
        part = jnp.sum(kernel_ref[0, k] * row_scale, axis=0, keepdims=True)
        d = dist_ref[b * MAXC + k]
        parts_ref[pl.ds(d, 1), :] += part


def spread(parts_ref, mass, out_ref):
    parts = parts_ref[...]
    for r in range(NR):
        out_ref[r, :ND, :] = parts
        out_ref[r, ND:, :] = mass


def scores_kernel(dist_ref, count_ref, *refs):
    rows_ref, weight_ref, mass_ref = refs[:3]
    lists = refs[3 : 3 + MAXC]
    kernel_ref, out_ref, parts_ref = refs[3 + MAXC :]
    b = pl.program_id(0)
    count = count_ref[b]
    rows = rows_ref[0]

    @pl.when(b == 0)
    def _():
        parts_ref[...] = jnp.zeros_like(parts_ref)

    total = jnp.zeros((RB, CB), F32)
    for k in range(0, MAXC, 2):
        pair = jnp.concatenate([lists[k][0], lists[k + 1][0]], axis=0)
        scores = lax.dot_general(
            rows, pair, (((1,), (1,)), ((), ())), preferred_element_type=F32
        )
        grown = jnp.exp(scores * (BETA / D))
        for n in range(2):
            live = jnp.where(k + n < count, grown[:, n * CB : (n + 1) * CB], 0.0)
            kernel_ref[0, k + n] = live
            total = total + live
    row_scale = weight_ref[0] / jnp.sum(total, axis=1, keepdims=True)
    column_pass(kernel_ref, row_scale, dist_ref, b, parts_ref)

    @pl.when(b == NBD - 1)
    def _():
        spread(parts_ref, mass_ref[...], out_ref)


def first_pass(dist, counts, rows, weights, mass, lists):
    fixed = lambda *shape: pl.BlockSpec(shape, lambda b, d, c: (0,) * len(shape))
    list_specs = [
        pl.BlockSpec((1, CB, D), lambda b, d, c, k=k: (d[b * MAXC + k], 0, 0)) for k in range(MAXC)
    ]
    return pl.pallas_call(
        scores_kernel,
        grid_spec=pltpu.PrefetchScalarGridSpec(
            num_scalar_prefetch=2,
            grid=(NBD,),
            in_specs=[
                pl.BlockSpec((1, RB, D), lambda b, d, c: (b, 0, 0)),
                pl.BlockSpec((1, RB, CB), lambda b, d, c: (b, 0, 0)),
                fixed(8, CB),
            ]
            + list_specs,
            out_specs=[
                pl.BlockSpec((1, MAXC, RB, CB), lambda b, d, c: (b, 0, 0, 0)),
                fixed(NR, NDX, CB),
            ],
            scratch_shapes=[pltpu.VMEM((ND, CB), F32)],
        ),
        out_shape=[
            jax.ShapeDtypeStruct((NBD, MAXC, RB, CB), F32),
            jax.ShapeDtypeStruct((NR, NDX, CB), F32),
        ],
        name="scores",
    )(dist, counts, rows, weights, mass, *([lists] * MAXC))


def new_scales(got_ref, same_ref, scales_ref):
    straight = jnp.zeros((ND, CB), F32)
    crossed = jnp.zeros((ND, CB), F32)
    mass = jnp.zeros((8, CB), F32)
    for r in range(NR):
        got = got_ref[r, :ND, :]
        straight = straight + same_ref[0, r] * got
        crossed = crossed + same_ref[1, r] * got
        mass = mass + got_ref[r, ND:, :]
    even = lax.broadcasted_iota(jnp.int32, (ND, CB), 0) % 2 == 0
    swapped = jnp.where(even, jnp.roll(crossed, -1, axis=0), jnp.roll(crossed, 1, axis=0))
    target = mass * (1.0 / K_TOTAL)
    column = straight + swapped
    scales_ref[...] = target[:1] / (column + PRIOR * target[:1])
    return target


def row_pass(kernel_ref, weight_ref, scales_ref, dist_ref, b):
    total = jnp.zeros((RB, CB), F32)
    for k in range(MAXC):
        d = dist_ref[b * MAXC + k]
        total = total + kernel_ref[0, k] * scales_ref[pl.ds(d, 1), :]
    return weight_ref[0] / jnp.sum(total, axis=1, keepdims=True)


def turn(dist, kernel, weights, got, same, mass):
    fixed = lambda *shape: pl.BlockSpec(shape, lambda b, d: (0,) * len(shape))

    def body(dist_ref, kernel_ref, weight_ref, got_ref, same_ref, mass_ref, out_ref, scales_ref, parts_ref):
        b = pl.program_id(0)

        @pl.when(b == 0)
        def _():
            new_scales(got_ref, same_ref, scales_ref)
            parts_ref[...] = jnp.zeros_like(parts_ref)

        row_scale = row_pass(kernel_ref, weight_ref, scales_ref, dist_ref, b)
        column_pass(kernel_ref, row_scale, dist_ref, b, parts_ref)

        @pl.when(b == NBD - 1)
        def _():
            spread(parts_ref, mass_ref[...], out_ref)

    return pl.pallas_call(
        body,
        grid_spec=pltpu.PrefetchScalarGridSpec(
            num_scalar_prefetch=1,
            grid=(NBD,),
            in_specs=[
                pl.BlockSpec((1, MAXC, RB, CB), lambda b, d: (b, 0, 0, 0)),
                pl.BlockSpec((1, RB, CB), lambda b, d: (b, 0, 0)),
                fixed(NR, NDX, CB),
                fixed(2, NR, ND, CB),
                fixed(8, CB),
            ],
            out_specs=fixed(NR, NDX, CB),
            scratch_shapes=[pltpu.VMEM((ND, CB), F32), pltpu.VMEM((ND, CB), F32)],
        ),
        out_shape=jax.ShapeDtypeStruct((NR, NDX, CB), F32),
        name="turn",
    )(dist, kernel, weights, got, same, mass)


def final_kernel(
    dist_ref,
    kernel_ref,
    weight_ref,
    rows_ref,
    got_ref,
    same_ref,
    out_ref,
    target_ref,
    scales_ref,
    parts_ref,
    rows_keep,
    plan_keep,
    order_ref,
    seen_ref,
):
    step = pl.program_id(0)

    @pl.when(step == 0)
    def _():
        target_ref[...] = new_scales(got_ref, same_ref, scales_ref)
        parts_ref[...] = jnp.zeros_like(parts_ref)

        @pl.loop(0, ND)
        def _(d):
            seen_ref[d] = 0

        @pl.loop(0, NBD * MAXC)
        def _(p):
            d = dist_ref[p]
            n = seen_ref[d]
            seen_ref[d] = n + 1
            holder = d // 2
            order_ref[holder * 4 + jnp.where(d % 2 == 0, n, 3 - n)] = p

    @pl.when(step < NBD)
    def _():
        b = step
        row_scale = row_pass(kernel_ref, weight_ref, scales_ref, dist_ref, b)
        for k in range(MAXC):
            d = dist_ref[b * MAXC + k]
            plan = row_scale * kernel_ref[0, k] * scales_ref[pl.ds(d, 1), :]
            parts_ref[pl.ds(d, 1), :] += jnp.sum(plan, axis=0, keepdims=True)
            plan_keep[b * MAXC + k] = jnp.transpose(plan).astype(BF16)
        rows_keep[b] = rows_ref[0]

    @pl.when(step >= NBD)
    def _():
        holder = step - NBD
        slots = [order_ref[holder * 4 + n] for n in range(4)]
        plans = [plan_keep[p] for p in slots]
        first = seen_ref[holder * 2]

        def emit(u, chosen):
            left = jnp.concatenate([plans[n] for n in chosen], axis=1)
            right = jnp.concatenate([rows_keep[slots[n] // MAXC] for n in chosen], axis=0)
            total = jnp.dot(left, right, preferred_element_type=F32)
            for c in range(D // 128):
                at = c * USE * CB + u * CB
                out_ref[0, at : at + CB, :] = total[:, c * 128 : (c + 1) * 128].astype(BF16)

        for split in (1, 2, 3):

            @pl.when(first == split)
            def _(split=split):
                emit(0, range(split))
                emit(1, range(split, 4))

        rest = parts_ref[pl.ds(holder * 2, 2), :]
        terms = []
        for _ in range(3):
            piece = rest.astype(BF16).astype(F32)
            terms.append(piece)
            rest = rest - piece
        terms.append(jnp.zeros((10, CB), F32))
        out_ref[0, ROWS_X:, :] = jnp.concatenate(terms, axis=0).astype(BF16)


def final_pass(dist, kernel, weights, rows, got, same):
    fixed = lambda *shape: pl.BlockSpec(shape, lambda s, d: (0,) * len(shape))
    early = lambda s: jnp.minimum(s, NBD - 1)
    return pl.pallas_call(
        final_kernel,
        grid_spec=pltpu.PrefetchScalarGridSpec(
            num_scalar_prefetch=1,
            grid=(NBD + NR,),
            in_specs=[
                pl.BlockSpec((1, MAXC, RB, CB), lambda s, d: (early(s), 0, 0, 0)),
                pl.BlockSpec((1, RB, CB), lambda s, d: (early(s), 0, 0)),
                pl.BlockSpec((1, RB, D), lambda s, d: (early(s), 0, 0)),
                fixed(NR, NDX, CB),
                fixed(2, NR, ND, CB),
            ],
            out_specs=[
                pl.BlockSpec((1, ROWS_P, 128), lambda s, d: (jnp.maximum(s - NBD, 0), 0, 0)),
                fixed(8, CB),
            ],
            scratch_shapes=[
                pltpu.VMEM((ND, CB), F32),
                pltpu.VMEM((ND, CB), F32),
                pltpu.VMEM((NBD, RB, D), BF16),
                pltpu.VMEM((NBD * MAXC, CB, RB), BF16),
                pltpu.SMEM((NBD * MAXC,), jnp.int32),
                pltpu.SMEM((ND,), jnp.int32),
            ],
        ),
        out_shape=[
            jax.ShapeDtypeStruct((NR, ROWS_P, 128), BF16),
            jax.ShapeDtypeStruct((8, CB), F32),
        ],
        name="final_pass",
    )(dist, kernel, weights, rows, got, same)


def merge_kernel(wanted_ref, got_ref, extra_ref, target_ref, out_ref, load_ref, order_ref, start_ref):
    step = pl.program_id(0)

    @pl.when(step == 0)
    def _():
        @pl.loop(0, CBD + 1)
        def _(j):
            start_ref[j] = 0

        @pl.loop(0, ND)
        def _(i):
            j = wanted_ref[i]
            start_ref[j + 1] = start_ref[j + 1] + 1

        @pl.loop(0, CBD)
        def _(j):
            start_ref[j + 1] = start_ref[j + 1] + start_ref[j]

        @pl.loop(0, ND)
        def _(n):
            i = ND - 1 - n
            j = wanted_ref[i]
            at = start_ref[j + 1] - 1
            start_ref[j + 1] = at
            order_ref[at] = i

        load_ref[...] = jnp.zeros_like(load_ref)
        for r in range(NR):
            terms = extra_ref[r].astype(F32)
            for u in range(USE):
                mass = terms[u : u + 1] + terms[u + 2 : u + 3] + terms[u + 4 : u + 5]
                load_ref[pl.ds(wanted_ref[r * USE + u], 1), :] += mass
        load_ref[...] = load_ref[...] / target_ref[:1]

    for j in range(CBD):
        begin = start_ref[j + 1]
        end = start_ref[j + 2] if j + 1 < CBD else ND

        def add(n, total):
            i = order_ref[n]
            at = pl.multiple_of((i % USE) * CB, CB)
            return total + got_ref[i // USE, pl.ds(at, CB), :].astype(F32)

        out_ref[j] = lax.fori_loop(begin, end, add, jnp.zeros((CB, 128), F32))


def merge(wanted, got, target):
    return pl.pallas_call(
        merge_kernel,
        grid_spec=pltpu.PrefetchScalarGridSpec(
            num_scalar_prefetch=1,
            grid=(D // 128,),
            in_specs=[
                pl.BlockSpec((NR, USE * CB, 128), lambda s, w: (0, s, 0)),
                pl.BlockSpec((NR, 16, 128), lambda s, w: (0, ROWS_X // 16, 0)),
                pl.BlockSpec((8, CB), lambda s, w: (0, 0)),
            ],
            out_specs=[
                pl.BlockSpec((CBD, CB, 128), lambda s, w: (0, 0, s)),
                pl.BlockSpec((CBD, CB), lambda s, w: (0, 0)),
            ],
            scratch_shapes=[pltpu.SMEM((ND,), jnp.int32), pltpu.SMEM((CBD + 2,), jnp.int32)],
        ),
        out_shape=[
            jax.ShapeDtypeStruct((CBD, CB, D), F32),
            jax.ShapeDtypeStruct((CBD, CB), F32),
        ],
        name="merge",
    )(wanted, got, got, target)


def exchange(values):
    return lax.all_to_all(values, "rows", split_axis=0, concat_axis=0, tiled=True)


def body(groups, centroids, row_weight, block_ids, block_counts):
    flat = block_ids.reshape(-1)
    holder = flat // (CBD * NC)
    local = flat % CBD
    of_holder = jnp.arange(NR, dtype=jnp.int32)[:, None] == holder[None, :]
    low = jnp.min(jnp.where(of_holder, local[None, :], CBD), axis=1)
    high = jnp.max(jnp.where(of_holder, local[None, :], -1), axis=1)
    table = jnp.stack([low, high], axis=1).reshape(1, 1, ND)
    tables = exchange(jnp.broadcast_to(table, (NR, 1, ND))).reshape(NR, ND)
    me = lax.axis_index("rows")
    wanted = lax.dynamic_slice(tables, (0, me * USE), (NR, USE)).reshape(-1)

    low_here = jnp.sum(jnp.where(of_holder, low[:, None], 0), axis=0)
    dist = holder * USE + (local != low_here).astype(jnp.int32)

    mass = jnp.broadcast_to(jnp.sum(row_weight), (8, CB))
    for bit in (1, 2, 4):
        mass = mass + lax.ppermute(mass, "cents", [(i, i ^ bit) for i in range(NC)])

    mine = table.reshape(ND)
    other = jnp.stack([high, low], axis=1).reshape(ND)
    same = jnp.stack([tables == mine[None, :], tables == other[None, :]]).astype(F32)
    same = jnp.broadcast_to(same[..., None], (2, NR, ND, CB))
    weights = jnp.broadcast_to(row_weight.reshape(NBD, RB, 1), (NBD, RB, CB))

    rows = normalize_rows(groups).reshape(NBD, RB, D)
    picked = pick_lists(centroids.reshape(CBD, CB, D), wanted).reshape(NR, USE * CB, D)
    picked, rows, weights, same, mass, dist = lax.optimization_barrier(
        (picked, rows, weights, same, mass, dist)
    )
    lists = exchange(picked).reshape(ND, CB, D)

    kernel, parts = first_pass(dist, block_counts, rows, weights, mass, lists)
    got = exchange(parts)
    for _ in range(ITERS - 1):
        got = exchange(turn(dist, kernel, weights, got, same, mass))
    sums, target = final_pass(dist, kernel, weights, rows, got, same)
    totals, load = merge(wanted, exchange(sums), target)
    return totals.reshape(-1, D), load.reshape(-1)


def solution(mesh):
    placed = (
        P(("rows", "cents"), None),
        P(("rows", "cents"), None),
        P(("rows", "cents")),
        P(("rows", "cents"), None),
        P(("rows", "cents")),
    )
    return jax.shard_map(
        body,
        mesh=mesh,
        in_specs=placed,
        out_specs=(P(("rows", "cents"), None), P(("rows", "cents"))),
        check_vma=False,
    )
```

```python
import jax
import jax.numpy as jnp
from jax import lax
from jax.experimental import pallas as pl
from jax.experimental.pallas import tpu as pltpu
from jax.sharding import PartitionSpec as P

D = 1024
RB = 256
CB = 128
MAXC = 8
USE = 2
ITERS = 3
NBD = 8
CBD = 16
NR = 16
NC = 8
ND = NR * USE
DEVICES = NR * NC
K_TOTAL = DEVICES * CBD * CB
ROWS_X = USE * CB * (D // 128)
ROWS_P = ROWS_X + 16

BETA = 32.0
EPSILON = 1e-06
PRIOR = 0.25
F32 = jnp.float32
BF16 = jnp.bfloat16
HELD = pl.BlockSpec(memory_space=pltpu.VMEM)
LIMIT = pltpu.CompilerParams(vmem_limit_bytes=40 << 20)


def unit_rows(values):
    widened = values.astype(F32)
    mean = jnp.sum(widened * widened, axis=-1, keepdims=True) * (1.0 / D)
    return (widened * lax.rsqrt(mean + EPSILON)).astype(BF16)


def table_kernel(ids_ref, weight_ref, table_ref, dist_ref, low_ref, high_ref):
    @pl.loop(0, NR)
    def _(o):
        low_ref[o] = CBD
        high_ref[o] = -1

    @pl.loop(0, NBD)
    def _(b):
        for k in range(MAXC):
            number = ids_ref[b, k]
            holder = number // (CBD * NC)
            local = number % CBD
            low_ref[holder] = jnp.minimum(low_ref[holder], local)
            high_ref[holder] = jnp.maximum(high_ref[holder], local)

    @pl.loop(0, NBD)
    def _(b):
        for k in range(MAXC):
            number = ids_ref[b, k]
            holder = number // (CBD * NC)
            local = number % CBD
            dist_ref[b * MAXC + k] = holder * USE + jnp.where(local != low_ref[holder], 1, 0)

    weight = jnp.sum(jnp.sum(weight_ref[...], axis=0, keepdims=True), axis=1, keepdims=True)
    lane = lax.broadcasted_iota(jnp.int32, (1, CB), 1)
    numbers = jnp.zeros((1, CB), jnp.int32)
    for o in range(NR):
        low = low_ref[o]
        high = high_ref[o]
        is_low = (lane == USE * o) | (lane == ND + USE * o + 1)
        is_high = (lane == USE * o + 1) | (lane == ND + USE * o)
        numbers = jnp.where(is_low, low, jnp.where(is_high, high, numbers))
    row = jnp.where(lane < 2 * ND, numbers.astype(F32), jnp.broadcast_to(weight, (1, CB)))
    table_ref[...] = jnp.broadcast_to(row, (DEVICES, CB))


def make_table(block_ids, weight_rows):
    return pl.pallas_call(
        table_kernel,
        in_specs=[pl.BlockSpec(memory_space=pltpu.SMEM), HELD],
        out_specs=[HELD, pl.BlockSpec(memory_space=pltpu.SMEM)],
        out_shape=[
            jax.ShapeDtypeStruct((DEVICES, CB), F32),
            jax.ShapeDtypeStruct((NBD * MAXC,), jnp.int32),
        ],
        scratch_shapes=[pltpu.SMEM((NR,), jnp.int32), pltpu.SMEM((NR,), jnp.int32)],
        name="make_table",
    )(block_ids, weight_rows)


def pick_kernel(wanted_ref, lists_ref, out_ref, order_ref, start_ref, raw, unit, raw_sem, out_sem):
    def load(j):
        return pltpu.make_async_copy(lists_ref.at[j], raw.at[j], raw_sem.at[j])

    def send(i):
        return pltpu.make_async_copy(unit.at[wanted_ref[i]], out_ref.at[i], out_sem.at[i])

    for j in range(CBD):
        load(j).start()

    @pl.loop(0, CBD + 2)
    def _(j):
        start_ref[j] = 0

    @pl.loop(0, ND)
    def _(i):
        j = wanted_ref[i]
        start_ref[j + 1] = start_ref[j + 1] + 1

    @pl.loop(0, CBD)
    def _(j):
        start_ref[j + 1] = start_ref[j + 1] + start_ref[j]

    @pl.loop(0, ND)
    def _(n):
        i = ND - 1 - n
        j = wanted_ref[i]
        at = start_ref[j + 1] - 1
        start_ref[j + 1] = at
        order_ref[at] = i

    start_ref[CBD + 1] = ND

    @pl.loop(0, CBD)
    def _(j):
        load(j).wait()
        unit[j] = unit_rows(raw[j])

        @pl.loop(start_ref[j + 1], start_ref[j + 2])
        def _(n):
            send(order_ref[n]).start()

    @pl.loop(0, ND)
    def _(i):
        send(i).wait()


def pick_lists(centroids, wanted):
    smem = pl.BlockSpec(memory_space=pltpu.SMEM)
    return pl.pallas_call(
        pick_kernel,
        in_specs=[smem, pl.BlockSpec(memory_space=pl.ANY)],
        out_specs=[pl.BlockSpec(memory_space=pl.ANY), smem, smem],
        out_shape=[
            jax.ShapeDtypeStruct((ND, CB, D), BF16),
            jax.ShapeDtypeStruct((ND,), jnp.int32),
            jax.ShapeDtypeStruct((CBD + 2,), jnp.int32),
        ],
        scratch_shapes=[
            pltpu.VMEM((CBD, CB, D), BF16),
            pltpu.VMEM((CBD, CB, D), BF16),
            pltpu.SemaphoreType.DMA((CBD,)),
            pltpu.SemaphoreType.DMA((ND,)),
        ],
        name="pick_lists",
    )(wanted, centroids)


def column_pass(kernel_ref, row_scale, dist_ref, b, parts_ref):
    for k in range(MAXC):
        part = jnp.sum(kernel_ref[b, k] * row_scale, axis=0, keepdims=True)
        d = dist_ref[b * MAXC + k]
        parts_ref[pl.ds(d, 1), :] += part


def spread(parts_ref, out_ref):
    parts = parts_ref[...]
    for r in range(NR):
        out_ref[r] = parts


def prepare(table_ref, spot_ref, same_ref, target_ref):
    rows = [table_ref[r, pl.ds(spot_ref[1], 1), :] for r in range(NR)]
    rows.append(table_ref[spot_ref[0], pl.ds(spot_ref[1], 1), :])
    rows.append(jnp.zeros((CB - NR - 1, CB), F32))
    turned = jnp.transpose(jnp.concatenate(rows, axis=0))
    mine = turned[:ND, NR : NR + 1]
    other = turned[ND : 2 * ND, NR : NR + 1]
    for r in range(NR):
        theirs = turned[:ND, r : r + 1]
        same_ref[0, r] = jnp.broadcast_to(jnp.where(theirs == mine, 1.0, 0.0), (ND, CB))
        same_ref[1, r] = jnp.broadcast_to(jnp.where(theirs == other, 1.0, 0.0), (ND, CB))
    total = jnp.sum(jnp.sum(table_ref[...], axis=0), axis=0, keepdims=True)
    lane = lax.broadcasted_iota(jnp.int32, (1, CB), 1)
    mass = jnp.sum(jnp.where(lane == CB - 1, total, 0.0), axis=1, keepdims=True)
    target_ref[...] = jnp.broadcast_to(mass * (1.0 / K_TOTAL), (8, CB))


def scores_kernel(dist_ref, count_ref, spot_ref, *refs):
    groups_ref, mass_ref, table_ref = refs[:3]
    lists = refs[3 : 3 + MAXC]
    kernel_ref, out_ref, same_ref, target_ref, rows_ref, weight_ref, parts_ref = refs[3 + MAXC :]
    b = pl.program_id(0)
    count = count_ref[b]

    @pl.when(b == 0)
    def _():
        parts_ref[...] = jnp.zeros_like(parts_ref)
        prepare(table_ref, spot_ref, same_ref, target_ref)

    rows = unit_rows(groups_ref[0])
    rows_ref[b] = rows
    for h in range(RB // CB):
        flat = jnp.broadcast_to(mass_ref[pl.ds(b * (RB // CB) + h, 1), :], (CB, CB))
        weight_ref[b, h * CB : (h + 1) * CB, :] = jnp.transpose(flat)

    total = jnp.zeros((RB, CB), F32)
    for k in range(0, MAXC, 2):
        pair = jnp.concatenate([lists[k][0], lists[k + 1][0]], axis=0)
        scores = lax.dot_general(
            rows, pair, (((1,), (1,)), ((), ())), preferred_element_type=F32
        )
        grown = jnp.exp(scores * (BETA / D))
        for n in range(2):
            live = jnp.where(k + n < count, grown[:, n * CB : (n + 1) * CB], 0.0)
            kernel_ref[b, k + n] = live
            total = total + live
    row_scale = weight_ref[b] / jnp.sum(total, axis=1, keepdims=True)
    column_pass(kernel_ref, row_scale, dist_ref, b, parts_ref)

    @pl.when(b == NBD - 1)
    def _():
        spread(parts_ref, out_ref)


def first_pass(dist, counts, spot, groups, weight_rows, table, lists):
    fixed = lambda *shape: pl.BlockSpec(shape, lambda b, d, c, p: (0,) * len(shape))
    list_specs = [
        pl.BlockSpec((1, CB, D), lambda b, d, c, p, k=k: (d[b * MAXC + k], 0, 0))
        for k in range(MAXC)
    ]
    return pl.pallas_call(
        scores_kernel,
        grid_spec=pltpu.PrefetchScalarGridSpec(
            num_scalar_prefetch=3,
            grid=(NBD,),
            in_specs=[pl.BlockSpec((1, RB, D), lambda b, d, c, p: (b, 0, 0)), HELD, HELD]
            + list_specs,
            out_specs=[HELD, fixed(NR, ND, CB), HELD, HELD, HELD, HELD],
            scratch_shapes=[pltpu.VMEM((ND, CB), F32)],
        ),
        out_shape=[
            pltpu.VMEM((NBD, MAXC, RB, CB), F32),
            jax.ShapeDtypeStruct((NR, ND, CB), F32),
            pltpu.VMEM((2, NR, ND, CB), F32),
            pltpu.VMEM((8, CB), F32),
            pltpu.VMEM((NBD, RB, D), BF16),
            pltpu.VMEM((NBD, RB, CB), F32),
        ],
        compiler_params=LIMIT,
        name="scores",
    )(dist, counts, spot, groups, weight_rows, table, *([lists] * MAXC))


def new_scales(got_ref, same_ref, target_ref, scales_ref):
    straight = jnp.zeros((ND, CB), F32)
    crossed = jnp.zeros((ND, CB), F32)
    for r in range(NR):
        got = got_ref[r]
        straight = straight + same_ref[0, r] * got
        crossed = crossed + same_ref[1, r] * got
    even = lax.broadcasted_iota(jnp.int32, (ND, CB), 0) % 2 == 0
    swapped = jnp.where(even, jnp.roll(crossed, -1, axis=0), jnp.roll(crossed, 1, axis=0))
    column = straight + swapped
    target = target_ref[:1]
    scales_ref[...] = target / (column + PRIOR * target)


def row_pass(kernel_ref, weight_ref, scales_ref, dist_ref, b):
    total = jnp.zeros((RB, CB), F32)
    for k in range(MAXC):
        d = dist_ref[b * MAXC + k]
        total = total + kernel_ref[b, k] * scales_ref[pl.ds(d, 1), :]
    return weight_ref[b] / jnp.sum(total, axis=1, keepdims=True)


def turn_kernel(
    dist_ref, kernel_ref, weight_ref, got_ref, same_ref, target_ref, out_ref, scales_ref, parts_ref
):
    b = pl.program_id(0)

    @pl.when(b == 0)
    def _():
        new_scales(got_ref, same_ref, target_ref, scales_ref)
        parts_ref[...] = jnp.zeros_like(parts_ref)

    row_scale = row_pass(kernel_ref, weight_ref, scales_ref, dist_ref, b)
    column_pass(kernel_ref, row_scale, dist_ref, b, parts_ref)

    @pl.when(b == NBD - 1)
    def _():
        spread(parts_ref, out_ref)


def turn(dist, kernel, weights, got, same, target):
    return pl.pallas_call(
        turn_kernel,
        grid_spec=pltpu.PrefetchScalarGridSpec(
            num_scalar_prefetch=1,
            grid=(NBD,),
            in_specs=[HELD] * 5,
            out_specs=HELD,
            scratch_shapes=[pltpu.VMEM((ND, CB), F32), pltpu.VMEM((ND, CB), F32)],
        ),
        out_shape=jax.ShapeDtypeStruct((NR, ND, CB), F32),
        compiler_params=LIMIT,
        name="turn",
    )(dist, kernel, weights, got, same, target)


def final_kernel(
    dist_ref,
    kernel_ref,
    weight_ref,
    rows_ref,
    got_ref,
    same_ref,
    target_ref,
    out_ref,
    scales_ref,
    parts_ref,
    plan_keep,
    order_ref,
    seen_ref,
):
    step = pl.program_id(0)

    @pl.when(step == 0)
    def _():
        new_scales(got_ref, same_ref, target_ref, scales_ref)
        parts_ref[...] = jnp.zeros_like(parts_ref)

        @pl.loop(0, ND)
        def _(d):
            seen_ref[d] = 0

        @pl.loop(0, NBD * MAXC)
        def _(p):
            d = dist_ref[p]
            n = seen_ref[d]
            seen_ref[d] = n + 1
            holder = d // 2
            order_ref[holder * 4 + jnp.where(d % 2 == 0, n, 3 - n)] = p

    @pl.when(step < NBD)
    def _():
        b = step
        row_scale = row_pass(kernel_ref, weight_ref, scales_ref, dist_ref, b)
        for k in range(MAXC):
            d = dist_ref[b * MAXC + k]
            plan = row_scale * kernel_ref[b, k] * scales_ref[pl.ds(d, 1), :]
            parts_ref[pl.ds(d, 1), :] += jnp.sum(plan, axis=0, keepdims=True)
            plan_keep[b * MAXC + k] = jnp.transpose(plan).astype(BF16)

    @pl.when(step >= NBD)
    def _():
        holder = step - NBD
        slots = [order_ref[holder * 4 + n] for n in range(4)]
        plans = [plan_keep[p] for p in slots]
        first = seen_ref[holder * 2]

        def emit(u, chosen):
            left = jnp.concatenate([plans[n] for n in chosen], axis=1)
            right = jnp.concatenate([rows_ref[slots[n] // MAXC] for n in chosen], axis=0)
            total = jnp.dot(left, right, preferred_element_type=F32)
            for c in range(D // 128):
                at = c * USE * CB + u * CB
                out_ref[0, at : at + CB, :] = total[:, c * 128 : (c + 1) * 128].astype(BF16)

        for split in (1, 2, 3):

            @pl.when(first == split)
            def _(split=split):
                emit(0, range(split))
                emit(1, range(split, 4))

        rest = parts_ref[pl.ds(holder * 2, 2), :]
        terms = []
        for _ in range(3):
            piece = rest.astype(BF16).astype(F32)
            terms.append(piece)
            rest = rest - piece
        terms.append(jnp.zeros((10, CB), F32))
        out_ref[0, ROWS_X:, :] = jnp.concatenate(terms, axis=0).astype(BF16)


def final_pass(dist, kernel, weights, rows, got, same, target):
    return pl.pallas_call(
        final_kernel,
        grid_spec=pltpu.PrefetchScalarGridSpec(
            num_scalar_prefetch=1,
            grid=(NBD + NR,),
            in_specs=[HELD] * 6,
            out_specs=pl.BlockSpec((1, ROWS_P, 128), lambda s, d: (jnp.maximum(s - NBD, 0), 0, 0)),
            scratch_shapes=[
                pltpu.VMEM((ND, CB), F32),
                pltpu.VMEM((ND, CB), F32),
                pltpu.VMEM((NBD * MAXC, CB, RB), BF16),
                pltpu.SMEM((NBD * MAXC,), jnp.int32),
                pltpu.SMEM((ND,), jnp.int32),
            ],
        ),
        out_shape=jax.ShapeDtypeStruct((NR, ROWS_P, 128), BF16),
        compiler_params=LIMIT,
        name="final_pass",
    )(dist, kernel, weights, rows, got, same, target)


def merge_kernel(
    wanted_ref, order_ref, start_ref, got_ref, target_ref, out_ref, load_ref, parts, extra, held, in_sem, out_sem
):
    chunks = D // 128

    def fetch(s):
        rows = pl.ds(pl.multiple_of(s * USE * CB, USE * CB), USE * CB)
        return pltpu.make_async_copy(got_ref.at[:, rows, :], parts.at[s], in_sem.at[s])

    def put(s):
        lanes = pl.ds(pl.multiple_of(s * 128, 128), 128)
        return pltpu.make_async_copy(held.at[s], out_ref.at[:, :, lanes], out_sem.at[s])

    for s in range(chunks):
        fetch(s).start()
    tail = pltpu.make_async_copy(got_ref.at[:, pl.ds(ROWS_X, 16), :], extra, in_sem.at[chunks])
    tail.start()

    @pl.loop(0, chunks)
    def _(s):
        fetch(s).wait()
        for j in range(CBD):

            def add(n, total):
                i = order_ref[n]
                at = pl.multiple_of((i % USE) * CB, CB)
                return total + parts[s, i // USE, pl.ds(at, CB), :].astype(F32)

            held[s, j] = lax.fori_loop(
                start_ref[j + 1], start_ref[j + 2], add, jnp.zeros((CB, 128), F32)
            )
        put(s).start()

    tail.wait()
    load_ref[...] = jnp.zeros_like(load_ref)
    for r in range(NR):
        terms = extra[r].astype(F32)
        for u in range(USE):
            mass = terms[u : u + 1] + terms[u + 2 : u + 3] + terms[u + 4 : u + 5]
            load_ref[pl.ds(wanted_ref[r * USE + u], 1), :] += mass
    load_ref[...] = load_ref[...] / target_ref[:1]

    @pl.loop(0, chunks)
    def _(s):
        put(s).wait()


def merge(wanted, order, start, got, target):
    smem = pl.BlockSpec(memory_space=pltpu.SMEM)
    chunks = D // 128
    return pl.pallas_call(
        merge_kernel,
        in_specs=[smem, smem, smem, pl.BlockSpec(memory_space=pl.ANY), HELD],
        out_specs=[pl.BlockSpec(memory_space=pl.ANY), HELD],
        scratch_shapes=[
            pltpu.VMEM((chunks, NR, USE * CB, 128), BF16),
            pltpu.VMEM((NR, 16, 128), BF16),
            pltpu.VMEM((chunks, CBD, CB, 128), F32),
            pltpu.SemaphoreType.DMA((chunks + 1,)),
            pltpu.SemaphoreType.DMA((chunks,)),
        ],
        out_shape=[
            jax.ShapeDtypeStruct((CBD, CB, D), F32),
            jax.ShapeDtypeStruct((CBD, CB), F32),
        ],
        name="merge",
    )(wanted, order, start, got, target)


def exchange(values):
    return lax.all_to_all(values, "rows", split_axis=0, concat_axis=0, tiled=True)


def body(groups, centroids, row_weight, block_ids, block_counts):
    weight_rows = row_weight.reshape(NBD * RB // CB, CB)
    table, dist = make_table(block_ids, weight_rows)
    me = lax.axis_index("rows")
    side = lax.axis_index("cents")
    spot = jnp.stack([me, side]).astype(jnp.int32)
    table, spot = lax.optimization_barrier((table, spot))
    tables = lax.all_to_all(
        table.reshape(DEVICES, 1, CB), ("rows", "cents"), split_axis=0, concat_axis=0, tiled=True
    ).reshape(NR, NC, CB)
    wanted = lax.dynamic_slice(tables, (0, spot[1], spot[0] * USE), (NR, 1, USE))
    wanted = wanted.reshape(-1).astype(jnp.int32)
    picked, order, start = pick_lists(centroids.reshape(CBD, CB, D), wanted)
    lists = exchange(picked.reshape(NR, USE * CB, D)).reshape(ND, CB, D)

    groups = groups.reshape(NBD, RB, D)
    kernel, parts, same, target, rows, weights = first_pass(
        dist, block_counts, spot, groups, weight_rows, tables, lists
    )
    got = exchange(parts)
    for _ in range(ITERS - 1):
        got = exchange(turn(dist, kernel, weights, got, same, target))
    sums = final_pass(dist, kernel, weights, rows, got, same, target)
    totals, load = merge(wanted, order, start, exchange(sums), target)
    return totals.reshape(-1, D), load.reshape(-1)


def solution(mesh):
    placed = (
        P(("rows", "cents"), None),
        P(("rows", "cents"), None),
        P(("rows", "cents")),
        P(("rows", "cents"), None),
        P(("rows", "cents")),
    )
    return jax.shard_map(
        body,
        mesh=mesh,
        in_specs=placed,
        out_specs=(P(("rows", "cents"), None), P(("rows", "cents"))),
        check_vma=False,
    )
```

```python
import jax
import jax.numpy as jnp
from jax import lax
from jax.experimental import pallas as pl
from jax.experimental.pallas import tpu as pltpu
from jax.sharding import PartitionSpec as P

D = 1024
RB = 256
CB = 128
MAXC = 8
USE = 2
ITERS = 3
NBD = 8
CBD = 16
NR = 16
NC = 8
ND = NR * USE
DEVICES = NR * NC
K_TOTAL = DEVICES * CBD * CB
ROWS_X = USE * CB * (D // 128)
ROWS_P = ROWS_X + 16

BETA = 32.0
EPSILON = 1e-06
PRIOR = 0.25
F32 = jnp.float32
BF16 = jnp.bfloat16
HELD = pl.BlockSpec(memory_space=pltpu.VMEM)
LIMIT = pltpu.CompilerParams(vmem_limit_bytes=20 << 20)


def unit_rows(values):
    widened = values.astype(F32)
    mean = jnp.sum(widened * widened, axis=-1, keepdims=True) * (1.0 / D)
    return (widened * lax.rsqrt(mean + EPSILON)).astype(BF16)


def table_kernel(ids_ref, weight_ref, table_ref, dist_ref, low_ref, high_ref):
    for o in range(NR):
        low_ref[o] = -1
        high_ref[o] = -1

    @pl.loop(0, NBD)
    def _(b):
        for k in range(MAXC):
            number = ids_ref[b, k]
            holder = number // (CBD * NC)
            local = number % CBD
            seen = low_ref[holder]
            low = jnp.where(seen < 0, local, seen)
            low_ref[holder] = low
            rank = jnp.where(local != low, 1, 0)
            high_ref[holder] = jnp.where(rank == 1, local, high_ref[holder])
            dist_ref[b * MAXC + k] = holder * USE + rank

    weight = jnp.sum(jnp.sum(weight_ref[...], axis=0, keepdims=True), axis=1, keepdims=True)
    lane = lax.broadcasted_iota(jnp.int32, (1, CB), 1)
    numbers = jnp.zeros((1, CB), jnp.int32)
    for o in range(NR):
        low = low_ref[o]
        high = high_ref[o]
        is_low = (lane == USE * o) | (lane == ND + USE * o + 1)
        is_high = (lane == USE * o + 1) | (lane == ND + USE * o)
        numbers = jnp.where(is_low, low, jnp.where(is_high, high, numbers))
    row = jnp.where(lane < 2 * ND, numbers.astype(F32), jnp.broadcast_to(weight, (1, CB)))
    table_ref[...] = jnp.broadcast_to(row, (DEVICES, CB))


def make_table(block_ids, weight_rows):
    return pl.pallas_call(
        table_kernel,
        in_specs=[pl.BlockSpec(memory_space=pltpu.SMEM), HELD],
        out_specs=[HELD, pl.BlockSpec(memory_space=pltpu.SMEM)],
        out_shape=[
            jax.ShapeDtypeStruct((DEVICES, CB), F32),
            jax.ShapeDtypeStruct((NBD * MAXC,), jnp.int32),
        ],
        scratch_shapes=[pltpu.SMEM((NR,), jnp.int32), pltpu.SMEM((NR,), jnp.int32)],
        name="make_table",
    )(block_ids, weight_rows)


def unit_kernel(lists_ref, groups_ref, unit_ref, rows_ref, raw, made, in_sem, out_sem):
    def span(n):
        return pl.ds(pl.multiple_of(n * CB, CB), CB)

    def load(source, n, at):
        return pltpu.make_async_copy(source.at[span(n)], raw.at[at], in_sem.at[at])

    def store(target, n, at):
        return pltpu.make_async_copy(made.at[at], target.at[span(n)], out_sem.at[at])

    pairs = ((lists_ref, unit_ref, 0), (groups_ref, rows_ref, CBD))
    for source, _, base in pairs:
        for n in range(CBD):
            load(source, n, base + n).start()
    for source, target, base in pairs:

        @pl.loop(0, CBD)
        def _(n, source=source, target=target, base=base):
            load(source, n, base + n).wait()
            made[base + n] = unit_rows(raw[base + n])
            store(target, n, base + n).start()

    for _, target, base in pairs:

        @pl.loop(0, CBD)
        def _(n, target=target, base=base):
            store(target, n, base + n).wait()


def unit_vectors(centroids, groups):
    far = pl.BlockSpec(memory_space=pl.ANY)
    return pl.pallas_call(
        unit_kernel,
        in_specs=[far, far],
        out_specs=[far, far],
        out_shape=[jax.ShapeDtypeStruct(centroids.shape, BF16), jax.ShapeDtypeStruct(groups.shape, BF16)],
        scratch_shapes=[
            pltpu.VMEM((2 * CBD, CB, D), BF16),
            pltpu.VMEM((2 * CBD, CB, D), BF16),
            pltpu.SemaphoreType.DMA((2 * CBD,)),
            pltpu.SemaphoreType.DMA((2 * CBD,)),
        ],
        cost_estimate=pl.CostEstimate(flops=1 << 24, bytes_accessed=1 << 24, transcendentals=1 << 12),
        name="unit_vectors",
    )(centroids, groups)


def prepare(rows, mine, tables_ref, same_ref, target_ref):
    filler = jnp.zeros((CB - NR - 1, CB), F32)
    turned = jnp.transpose(jnp.concatenate([rows, mine, filler], axis=0))
    here = turned[:ND, NR : NR + 1]
    other = turned[ND : 2 * ND, NR : NR + 1]
    for r in range(NR):
        theirs = turned[:ND, r : r + 1]
        same_ref[0, r] = jnp.broadcast_to(jnp.where(theirs == here, 1.0, 0.0), (ND, CB))
        same_ref[1, r] = jnp.broadcast_to(jnp.where(theirs == other, 1.0, 0.0), (ND, CB))
    total = jnp.sum(jnp.sum(tables_ref[...], axis=0), axis=0, keepdims=True)
    lane = lax.broadcasted_iota(jnp.int32, (1, CB), 1)
    mass = jnp.sum(jnp.where(lane == CB - 1, total, 0.0), axis=1, keepdims=True)
    target_ref[...] = jnp.broadcast_to(mass * (1.0 / K_TOTAL), (8, CB))


def pick_kernel(
    tables_ref,
    table_ref,
    lists_ref,
    out_ref,
    wanted_ref,
    same_ref,
    target_ref,
    numbers,
    scalars,
    unit,
    in_sem,
    move_sem,
):
    me = lax.axis_index("rows")
    side = lax.axis_index("cents")

    def load(j):
        return pltpu.make_async_copy(lists_ref.at[j], unit.at[j], in_sem.at[j])

    for j in range(CBD):
        load(j).start()
    rows = jnp.concatenate([tables_ref[r, pl.ds(side, 1), :] for r in range(NR)], axis=0)
    numbers[...] = rows.astype(jnp.int32)
    move = pltpu.make_async_copy(numbers, scalars, move_sem)
    move.start()
    prepare(rows, table_ref[:1], tables_ref, same_ref, target_ref)
    move.wait()
    for j in range(CBD):
        load(j).wait()

    @pl.loop(0, NR)
    def _(r):
        for u in range(USE):
            j = scalars[r, me * USE + u]
            wanted_ref[r * USE + u] = j
            out_ref[r * USE + u] = unit[j]


def pick_lists(tables, table, unit):
    return pl.pallas_call(
        pick_kernel,
        in_specs=[HELD, HELD, pl.BlockSpec(memory_space=pl.ANY)],
        out_specs=[HELD, pl.BlockSpec(memory_space=pltpu.SMEM), HELD, HELD],
        out_shape=[
            pltpu.VMEM((ND, CB, D), BF16),
            jax.ShapeDtypeStruct((ND,), jnp.int32),
            pltpu.VMEM((2, NR, ND, CB), F32),
            pltpu.VMEM((8, CB), F32),
        ],
        scratch_shapes=[
            pltpu.VMEM((NR, CB), jnp.int32),
            pltpu.SMEM((NR, CB), jnp.int32),
            pltpu.VMEM((CBD, CB, D), BF16),
            pltpu.SemaphoreType.DMA((CBD,)),
            pltpu.SemaphoreType.DMA,
        ],
        compiler_params=pltpu.CompilerParams(vmem_limit_bytes=54 << 20),
        name="pick_lists",
    )(tables, table, unit)


def column_pass(kernel_ref, row_scale, dist_ref, b, parts_ref):
    for k in range(MAXC):
        part = jnp.sum(kernel_ref[b, k] * row_scale, axis=0, keepdims=True)
        d = dist_ref[b * MAXC + k]
        parts_ref[pl.ds(d, 1), :] += part


def spread(parts_ref, out_ref):
    parts = parts_ref[...]
    for r in range(NR):
        out_ref[r] = parts


STEP = 2


def scores_kernel(dist_ref, count_ref, *refs):
    rows_ref, mass_ref, lists_ref, kernel_ref, out_ref, weight_ref, parts_ref = refs
    step = pl.program_id(0)

    @pl.when(step == 0)
    def _():
        parts_ref[...] = jnp.zeros_like(parts_ref)

    for n in range(STEP):
        b = step * STEP + n
        count = count_ref[b]
        rows = rows_ref[b]
        halves = []
        for h in range(RB // CB):
            flat = jnp.broadcast_to(mass_ref[pl.ds(b * (RB // CB) + h, 1), :], (CB, CB))
            halves.append(jnp.transpose(flat))
        weight = jnp.concatenate(halves, axis=0)
        weight_ref[b] = weight
        total = jnp.zeros((RB, CB), F32)
        for k in range(0, MAXC, 2):
            named = [dist_ref[b * MAXC + k + m] for m in range(2)]
            pair = jnp.concatenate([lists_ref[d] for d in named], axis=0)
            scores = lax.dot_general(
                rows, pair, (((1,), (1,)), ((), ())), preferred_element_type=F32
            )
            grown = jnp.exp(scores * (BETA / D))
            for m in range(2):
                live = jnp.where(k + m < count, grown[:, m * CB : (m + 1) * CB], 0.0)
                kernel_ref[b, k + m] = live
                total = total + live
        row_scale = weight / jnp.sum(total, axis=1, keepdims=True)
        column_pass(kernel_ref, row_scale, dist_ref, b, parts_ref)

    @pl.when(step == NBD // STEP - 1)
    def _():
        spread(parts_ref, out_ref)


def first_pass(dist, counts, rows, weight_rows, lists):
    return pl.pallas_call(
        scores_kernel,
        grid_spec=pltpu.PrefetchScalarGridSpec(
            num_scalar_prefetch=2,
            grid=(NBD // STEP,),
            in_specs=[HELD] * 3,
            out_specs=[HELD] * 3,
            scratch_shapes=[pltpu.VMEM((ND, CB), F32)],
        ),
        out_shape=[
            pltpu.VMEM((NBD, MAXC, RB, CB), F32),
            jax.ShapeDtypeStruct((NR, ND, CB), F32),
            pltpu.VMEM((NBD, RB, CB), F32),
        ],
        compiler_params=LIMIT,
        name="scores",
    )(dist, counts, rows, weight_rows, lists)


def new_scales(got_ref, same_ref, target_ref, scales_ref):
    straight = jnp.zeros((ND, CB), F32)
    crossed = jnp.zeros((ND, CB), F32)
    for r in range(NR):
        got = got_ref[r]
        straight = straight + same_ref[0, r] * got
        crossed = crossed + same_ref[1, r] * got
    even = lax.broadcasted_iota(jnp.int32, (ND, CB), 0) % 2 == 0
    swapped = jnp.where(even, jnp.roll(crossed, -1, axis=0), jnp.roll(crossed, 1, axis=0))
    column = straight + swapped
    target = target_ref[:1]
    scales_ref[...] = target / (column + PRIOR * target)


def row_pass(kernel_ref, weight_ref, scales_ref, dist_ref, b):
    total = jnp.zeros((RB, CB), F32)
    for k in range(MAXC):
        d = dist_ref[b * MAXC + k]
        total = total + kernel_ref[b, k] * scales_ref[pl.ds(d, 1), :]
    return weight_ref[b] / jnp.sum(total, axis=1, keepdims=True)


def turn_kernel(
    dist_ref, kernel_ref, weight_ref, got_ref, same_ref, target_ref, out_ref, scales_ref, parts_ref
):
    b = pl.program_id(0)

    @pl.when(b == 0)
    def _():
        new_scales(got_ref, same_ref, target_ref, scales_ref)
        parts_ref[...] = jnp.zeros_like(parts_ref)

    row_scale = row_pass(kernel_ref, weight_ref, scales_ref, dist_ref, b)
    column_pass(kernel_ref, row_scale, dist_ref, b, parts_ref)

    @pl.when(b == NBD - 1)
    def _():
        spread(parts_ref, out_ref)


def turn(dist, kernel, weights, got, same, target):
    return pl.pallas_call(
        turn_kernel,
        grid_spec=pltpu.PrefetchScalarGridSpec(
            num_scalar_prefetch=1,
            grid=(NBD,),
            in_specs=[HELD] * 5,
            out_specs=HELD,
            scratch_shapes=[pltpu.VMEM((ND, CB), F32), pltpu.VMEM((ND, CB), F32)],
        ),
        out_shape=jax.ShapeDtypeStruct((NR, ND, CB), F32),
        compiler_params=LIMIT,
        name="turn",
    )(dist, kernel, weights, got, same, target)


def final_kernel(
    dist_ref,
    kernel_ref,
    weight_ref,
    rows_ref,
    got_ref,
    same_ref,
    target_ref,
    out_ref,
    scales_ref,
    parts_ref,
    plan_keep,
    order_ref,
    seen_ref,
):
    step = pl.program_id(0)

    @pl.when(step == 0)
    def _():
        new_scales(got_ref, same_ref, target_ref, scales_ref)
        parts_ref[...] = jnp.zeros_like(parts_ref)

        for d in range(ND):
            seen_ref[d] = 0

    @pl.when(step < NBD)
    def _():
        b = step
        row_scale = row_pass(kernel_ref, weight_ref, scales_ref, dist_ref, b)
        for k in range(MAXC):
            d = dist_ref[b * MAXC + k]
            plan = row_scale * kernel_ref[b, k] * scales_ref[pl.ds(d, 1), :]
            parts_ref[pl.ds(d, 1), :] += jnp.sum(plan, axis=0, keepdims=True)
            plan_keep[b * MAXC + k] = jnp.transpose(plan.astype(BF16))
            n = seen_ref[d]
            seen_ref[d] = n + 1
            order_ref[d // 2 * 4 + jnp.where(d % 2 == 0, n, 3 - n)] = b * MAXC + k

    @pl.when(step >= NBD)
    def _():
        holder = step - NBD
        slots = [order_ref[holder * 4 + n] for n in range(4)]
        plans = [plan_keep[p] for p in slots]
        first = seen_ref[holder * 2]

        def emit(u, chosen):
            left = jnp.concatenate([plans[n] for n in chosen], axis=1)
            right = jnp.concatenate([rows_ref[slots[n] // MAXC] for n in chosen], axis=0)
            total = jnp.dot(left, right, preferred_element_type=F32)
            for c in range(D // 128):
                at = c * USE * CB + u * CB
                out_ref[holder, at : at + CB, :] = total[:, c * 128 : (c + 1) * 128].astype(BF16)

        for split in (1, 2, 3):

            @pl.when(first == split)
            def _(split=split):
                emit(0, range(split))
                emit(1, range(split, 4))

        rest = parts_ref[pl.ds(holder * 2, 2), :]
        terms = []
        for _ in range(3):
            piece = rest.astype(BF16).astype(F32)
            terms.append(piece)
            rest = rest - piece
        terms.append(jnp.zeros((10, CB), F32))
        out_ref[holder, ROWS_X:, :] = jnp.concatenate(terms, axis=0).astype(BF16)


def final_pass(dist, kernel, weights, rows, got, same, target):
    return pl.pallas_call(
        final_kernel,
        grid_spec=pltpu.PrefetchScalarGridSpec(
            num_scalar_prefetch=1,
            grid=(NBD + NR,),
            in_specs=[HELD] * 6,
            out_specs=HELD,
            scratch_shapes=[
                pltpu.VMEM((ND, CB), F32),
                pltpu.VMEM((ND, CB), F32),
                pltpu.VMEM((NBD * MAXC, CB, RB), BF16),
                pltpu.SMEM((NBD * MAXC,), jnp.int32),
                pltpu.SMEM((ND,), jnp.int32),
            ],
        ),
        out_shape=pltpu.VMEM((NR, ROWS_P, 128), BF16),
        compiler_params=LIMIT,
        name="final_pass",
    )(dist, kernel, weights, rows, got, same, target)


def merge_kernel(
    wanted_ref, got_ref, target_ref, out_ref, load_ref, held, order_ref, start_ref, out_sem
):
    chunks = D // 128

    def put(s):
        lanes = pl.ds(pl.multiple_of(s * 128, 128), 128)
        return pltpu.make_async_copy(held.at[s], out_ref.at[:, :, lanes], out_sem.at[s])

    for j in range(CBD + 2):
        start_ref[j] = 0

    @pl.loop(0, ND)
    def _(i):
        j = wanted_ref[i]
        start_ref[j + 1] = start_ref[j + 1] + 1

    @pl.loop(0, CBD)
    def _(j):
        begin = start_ref[j]
        count = start_ref[j + 1]
        start_ref[j + 1] = begin + count

        @pl.when(count == 0)
        def _():
            for s in range(chunks):
                held[s, j] = jnp.zeros((CB, 128), F32)

    @pl.loop(0, ND)
    def _(i):
        j = wanted_ref[i]
        at = start_ref[j]
        start_ref[j] = at + 1
        order_ref[at] = i

    @pl.loop(0, chunks)
    def _(s):
        total = jnp.zeros((CB, 128), F32)
        last = -1
        for n in range(ND):
            i = order_ref[n]
            j = wanted_ref[i]
            at = pl.multiple_of(s * (USE * CB) + (i % USE) * CB, CB)
            part = got_ref[i // USE, pl.ds(at, CB), :].astype(F32)
            total = part + jnp.where(j == last, total, 0.0)
            held[s, j] = total
            last = j
        put(s).start()

    load_ref[...] = jnp.zeros_like(load_ref)
    for r in range(NR):
        terms = got_ref[r, ROWS_X:, :].astype(F32)
        for u in range(USE):
            mass = terms[u : u + 1] + terms[u + 2 : u + 3] + terms[u + 4 : u + 5]
            load_ref[pl.ds(wanted_ref[r * USE + u], 1), :] += mass
    load_ref[...] = load_ref[...] / target_ref[:1]

    @pl.loop(0, chunks)
    def _(s):
        put(s).wait()


def merge(wanted, got, target):
    chunks = D // 128
    return pl.pallas_call(
        merge_kernel,
        in_specs=[pl.BlockSpec(memory_space=pltpu.SMEM), HELD, HELD],
        out_specs=[pl.BlockSpec(memory_space=pl.ANY), HELD],
        scratch_shapes=[
            pltpu.VMEM((chunks, CBD, CB, 128), F32),
            pltpu.SMEM((ND,), jnp.int32),
            pltpu.SMEM((CBD + 2,), jnp.int32),
            pltpu.SemaphoreType.DMA((chunks,)),
        ],
        out_shape=[
            jax.ShapeDtypeStruct((CBD, CB, D), F32),
            jax.ShapeDtypeStruct((CBD, CB), F32),
        ],
        compiler_params=LIMIT,
        name="merge",
    )(wanted, got, target)


def exchange(values):
    return lax.all_to_all(values, "rows", split_axis=0, concat_axis=0, tiled=True)


def body(groups, centroids, row_weight, block_ids, block_counts):
    weight_rows = row_weight.reshape(NBD * RB // CB, CB)
    table, dist = make_table(block_ids, weight_rows)
    tables = lax.all_to_all(
        table.reshape(DEVICES, 1, CB), ("rows", "cents"), split_axis=0, concat_axis=0, tiled=True
    ).reshape(NR, NC, CB)
    unit, rows = unit_vectors(centroids, groups)
    picked, wanted, same, target = pick_lists(
        tables, table, unit.reshape(CBD, CB, D)
    )
    rows = rows.reshape(NBD, RB, D)
    lists = exchange(picked.reshape(NR, USE * CB, D)).reshape(ND, CB, D)

    kernel, parts, weights = first_pass(dist, block_counts, rows, weight_rows, lists)
    got = exchange(parts)
    for _ in range(ITERS - 1):
        got = exchange(turn(dist, kernel, weights, got, same, target))
    sums = final_pass(dist, kernel, weights, rows, got, same, target)
    totals, load = merge(wanted, exchange(sums), target)
    return totals.reshape(-1, D), load.reshape(-1)


def solution(mesh):
    placed = (
        P(("rows", "cents"), None),
        P(("rows", "cents"), None),
        P(("rows", "cents")),
        P(("rows", "cents"), None),
        P(("rows", "cents")),
    )
    return jax.shard_map(
        body,
        mesh=mesh,
        in_specs=placed,
        out_specs=(P(("rows", "cents"), None), P(("rows", "cents"))),
        check_vma=False,
    )
```

```python
import jax
import jax.numpy as jnp
from jax import lax
from jax.experimental import pallas as pl
from jax.experimental.pallas import tpu as pltpu
from jax.sharding import PartitionSpec as P

D = 1024
RB = 256
CB = 128
MAXC = 8
USE = 2
ITERS = 3
NBD = 8
CBD = 16
NR = 16
NC = 8
ND = NR * USE
DEVICES = NR * NC
K_TOTAL = DEVICES * CBD * CB
ROWS_X = USE * CB * (D // 128)
ROWS_P = ROWS_X + 16
HOLDER_BITS = (CBD * NC).bit_length() - 1

BETA = 32.0
EPSILON = 1e-06
PRIOR = 0.25
F32 = jnp.float32
BF16 = jnp.bfloat16
HELD = pl.BlockSpec(memory_space=pltpu.VMEM)
LIMIT = pltpu.CompilerParams(vmem_limit_bytes=20 << 20)


def unit_rows(values):
    widened = values.astype(F32)
    mean = jnp.sum(widened * widened, axis=-1, keepdims=True) * (1.0 / D)
    return (widened * lax.rsqrt(mean + EPSILON)).astype(BF16)


def table_kernel(
    ids_ref, weight_ref, lists_ref, table_ref, dist_ref, unit_ref, low_ref, high_ref, raw, sem
):
    def load(n):
        return pltpu.make_async_copy(lists_ref.at[n], raw.at[n], sem.at[n])

    for n in range(CBD):
        load(n).start()
    for o in range(NR):
        low_ref[o] = -1
        high_ref[o] = -1
    part = MAXC // 2

    @pl.loop(0, CBD)
    def _(n):
        load(n).wait()
        for m in range(part):
            b = n >> 1
            k = (n & 1) * part + m
            number = ids_ref[b, k]
            holder = number >> HOLDER_BITS
            local = number & (CBD - 1)
            seen = low_ref[holder]
            low = jnp.where(seen < 0, local, seen)
            low_ref[holder] = low
            rank = jnp.where(local != low, 1, 0)
            high_ref[holder] = jnp.where(rank == 1, local, high_ref[holder])
            dist_ref[n * part + m] = holder * USE + rank
        unit_ref[n] = unit_rows(raw[n])

    weight = jnp.sum(jnp.sum(weight_ref[...], axis=0, keepdims=True), axis=1, keepdims=True)
    lane = lax.broadcasted_iota(jnp.int32, (1, CB), 1)
    numbers = jnp.zeros((1, CB), jnp.int32)
    for o in range(NR):
        low = low_ref[o]
        high = high_ref[o]
        is_low = (lane == USE * o) | (lane == ND + USE * o + 1)
        is_high = (lane == USE * o + 1) | (lane == ND + USE * o)
        numbers = jnp.where(is_low, low, jnp.where(is_high, high, numbers))
    row = jnp.where(lane < 2 * ND, numbers.astype(F32), jnp.broadcast_to(weight, (1, CB)))
    table_ref[...] = jnp.broadcast_to(row, (DEVICES, CB))


def make_table(block_ids, weight_rows, centroids):
    smem = pl.BlockSpec(memory_space=pltpu.SMEM)
    return pl.pallas_call(
        table_kernel,
        in_specs=[smem, HELD, pl.BlockSpec(memory_space=pl.ANY)],
        out_specs=[HELD, smem, HELD],
        out_shape=[
            pltpu.VMEM((DEVICES, CB), F32),
            jax.ShapeDtypeStruct((NBD * MAXC,), jnp.int32),
            pltpu.VMEM((CBD, CB, D), BF16),
        ],
        scratch_shapes=[
            pltpu.SMEM((NR,), jnp.int32),
            pltpu.SMEM((NR,), jnp.int32),
            pltpu.VMEM((CBD, CB, D), BF16),
            pltpu.SemaphoreType.DMA((CBD,)),
        ],
        compiler_params=pltpu.CompilerParams(vmem_limit_bytes=57 << 20),
        name="make_table",
    )(block_ids, weight_rows, centroids)


def prepare(rows, mine, tables_ref, same_ref, target_ref):
    filler = jnp.zeros((CB - NR - 1, CB), F32)
    turned = jnp.transpose(jnp.concatenate([rows, mine, filler], axis=0))
    here = turned[:ND, NR : NR + 1]
    other = turned[ND : 2 * ND, NR : NR + 1]
    for r in range(NR):
        theirs = turned[:ND, r : r + 1]
        same_ref[0, r] = jnp.broadcast_to(jnp.where(theirs == here, 1.0, 0.0), (ND, CB))
        same_ref[1, r] = jnp.broadcast_to(jnp.where(theirs == other, 1.0, 0.0), (ND, CB))
    total = jnp.sum(jnp.sum(tables_ref[...], axis=0), axis=0, keepdims=True)
    lane = lax.broadcasted_iota(jnp.int32, (1, CB), 1)
    mass = jnp.sum(jnp.where(lane == CB - 1, total, 0.0), axis=1, keepdims=True)
    target_ref[...] = jnp.broadcast_to(mass * (1.0 / K_TOTAL), (8, CB))


def pick_kernel(
    tables_ref,
    table_ref,
    lists_ref,
    out_ref,
    wanted_ref,
    same_ref,
    target_ref,
    numbers,
    scalars,
    move_sem,
):
    me = lax.axis_index("rows")
    side = lax.axis_index("cents")

    rows = jnp.concatenate([tables_ref[r, pl.ds(side, 1), :] for r in range(NR)], axis=0)
    numbers[...] = rows.astype(jnp.int32)
    move = pltpu.make_async_copy(numbers, scalars, move_sem)
    move.start()
    prepare(rows, table_ref[:1], tables_ref, same_ref, target_ref)

    move.wait()

    @pl.loop(0, NR)
    def _(r):
        for u in range(USE):
            j = scalars[r, me * USE + u]
            wanted_ref[r * USE + u] = j
            out_ref[r * USE + u] = lists_ref[j]


def pick_lists(tables, table, unit):
    return pl.pallas_call(
        pick_kernel,
        in_specs=[HELD, HELD, HELD],
        out_specs=[HELD, pl.BlockSpec(memory_space=pltpu.SMEM), HELD, HELD],
        out_shape=[
            pltpu.VMEM((ND, CB, D), BF16),
            jax.ShapeDtypeStruct((ND,), jnp.int32),
            pltpu.VMEM((2, NR, ND, CB), F32),
            pltpu.VMEM((8, CB), F32),
        ],
        scratch_shapes=[
            pltpu.VMEM((NR, CB), jnp.int32),
            pltpu.SMEM((NR, CB), jnp.int32),
            pltpu.SemaphoreType.DMA,
        ],
        compiler_params=LIMIT,
        name="pick_lists",
    )(tables, table, unit)


def column_pass(kernel_ref, row_scale, dist_ref, b, parts_ref):
    for k in range(MAXC):
        part = jnp.sum(kernel_ref[b, k] * row_scale, axis=0, keepdims=True)
        d = dist_ref[b * MAXC + k]
        parts_ref[pl.ds(d, 1), :] += part


def spread(parts_ref, out_ref):
    parts = parts_ref[...]
    for r in range(NR):
        out_ref[r] = parts


STEP = 2


def scores_kernel(dist_ref, count_ref, *refs):
    groups_ref, mass_ref, lists_ref, kernel_ref, out_ref, rows_ref, weight_ref, parts_ref = refs
    step = pl.program_id(0)

    @pl.when(step == 0)
    def _():
        parts_ref[...] = jnp.zeros_like(parts_ref)

    for n in range(STEP):
        b = step * STEP + n
        count = count_ref[b]
        rows = unit_rows(groups_ref[b])
        rows_ref[b] = rows
        halves = []
        for h in range(RB // CB):
            flat = jnp.broadcast_to(mass_ref[pl.ds(b * (RB // CB) + h, 1), :], (CB, CB))
            halves.append(jnp.transpose(flat))
        weight = jnp.concatenate(halves, axis=0)
        weight_ref[b] = weight
        total = jnp.zeros((RB, CB), F32)
        for k in range(0, MAXC, 2):
            named = [dist_ref[b * MAXC + k + m] for m in range(2)]
            pair = jnp.concatenate([lists_ref[d] for d in named], axis=0)
            scores = lax.dot_general(
                rows, pair, (((1,), (1,)), ((), ())), preferred_element_type=F32
            )
            grown = jnp.exp(scores * (BETA / D))
            for m in range(2):
                live = jnp.where(k + m < count, grown[:, m * CB : (m + 1) * CB], 0.0)
                kernel_ref[b, k + m] = live
                total = total + live
        row_scale = weight / jnp.sum(total, axis=1, keepdims=True)
        column_pass(kernel_ref, row_scale, dist_ref, b, parts_ref)

    @pl.when(step == NBD // STEP - 1)
    def _():
        spread(parts_ref, out_ref)


def first_pass(dist, counts, groups, weight_rows, lists):
    return pl.pallas_call(
        scores_kernel,
        grid_spec=pltpu.PrefetchScalarGridSpec(
            num_scalar_prefetch=2,
            grid=(NBD // STEP,),
            in_specs=[HELD] * 3,
            out_specs=[HELD] * 4,
            scratch_shapes=[pltpu.VMEM((ND, CB), F32)],
        ),
        out_shape=[
            pltpu.VMEM((NBD, MAXC, RB, CB), F32),
            jax.ShapeDtypeStruct((NR, ND, CB), F32),
            pltpu.VMEM((NBD, RB, D), BF16),
            pltpu.VMEM((NBD, RB, CB), F32),
        ],
        compiler_params=LIMIT,
        name="scores",
    )(dist, counts, groups, weight_rows, lists)


def new_scales(got_ref, same_ref, target_ref, scales_ref):
    straight = jnp.zeros((ND, CB), F32)
    crossed = jnp.zeros((ND, CB), F32)
    for r in range(NR):
        got = got_ref[r]
        straight = straight + same_ref[0, r] * got
        crossed = crossed + same_ref[1, r] * got
    even = lax.broadcasted_iota(jnp.int32, (ND, CB), 0) % 2 == 0
    swapped = jnp.where(even, jnp.roll(crossed, -1, axis=0), jnp.roll(crossed, 1, axis=0))
    column = straight + swapped
    target = target_ref[:1]
    scales_ref[...] = target / (column + PRIOR * target)


def row_pass(kernel_ref, weight_ref, scales_ref, dist_ref, b):
    total = jnp.zeros((RB, CB), F32)
    for k in range(MAXC):
        d = dist_ref[b * MAXC + k]
        total = total + kernel_ref[b, k] * scales_ref[pl.ds(d, 1), :]
    return weight_ref[b] / jnp.sum(total, axis=1, keepdims=True)


def turn_kernel(
    dist_ref, kernel_ref, weight_ref, got_ref, same_ref, target_ref, out_ref, scales_ref, parts_ref
):
    b = pl.program_id(0)

    @pl.when(b == 0)
    def _():
        new_scales(got_ref, same_ref, target_ref, scales_ref)
        parts_ref[...] = jnp.zeros_like(parts_ref)

    row_scale = row_pass(kernel_ref, weight_ref, scales_ref, dist_ref, b)
    column_pass(kernel_ref, row_scale, dist_ref, b, parts_ref)

    @pl.when(b == NBD - 1)
    def _():
        spread(parts_ref, out_ref)


def turn(dist, kernel, weights, got, same, target):
    return pl.pallas_call(
        turn_kernel,
        grid_spec=pltpu.PrefetchScalarGridSpec(
            num_scalar_prefetch=1,
            grid=(NBD,),
            in_specs=[HELD] * 5,
            out_specs=HELD,
            scratch_shapes=[pltpu.VMEM((ND, CB), F32), pltpu.VMEM((ND, CB), F32)],
        ),
        out_shape=jax.ShapeDtypeStruct((NR, ND, CB), F32),
        compiler_params=LIMIT,
        name="turn",
    )(dist, kernel, weights, got, same, target)


def final_kernel(
    dist_ref,
    kernel_ref,
    weight_ref,
    rows_ref,
    got_ref,
    same_ref,
    target_ref,
    out_ref,
    scales_ref,
    parts_ref,
    plan_keep,
    order_ref,
    seen_ref,
):
    step = pl.program_id(0)

    @pl.when(step == 0)
    def _():
        new_scales(got_ref, same_ref, target_ref, scales_ref)
        parts_ref[...] = jnp.zeros_like(parts_ref)

        for d in range(ND):
            seen_ref[d] = 0

    @pl.when(step < NBD)
    def _():
        b = step
        row_scale = row_pass(kernel_ref, weight_ref, scales_ref, dist_ref, b)
        for k in range(MAXC):
            d = dist_ref[b * MAXC + k]
            plan = row_scale * kernel_ref[b, k] * scales_ref[pl.ds(d, 1), :]
            parts_ref[pl.ds(d, 1), :] += jnp.sum(plan, axis=0, keepdims=True)
            plan_keep[b * MAXC + k] = jnp.transpose(plan.astype(BF16))
            n = seen_ref[d]
            seen_ref[d] = n + 1
            order_ref[(d >> 1) * 4 + jnp.where(d & 1 == 0, n, 3 - n)] = b * MAXC + k

    @pl.when(step >= NBD)
    def _():
        holder = step - NBD
        slots = [order_ref[holder * 4 + n] for n in range(4)]
        plans = [plan_keep[p] for p in slots]
        first = seen_ref[holder * 2]

        def emit(u, chosen):
            left = jnp.concatenate([plans[n] for n in chosen], axis=1)
            right = jnp.concatenate([rows_ref[slots[n] >> 3] for n in chosen], axis=0)
            total = jnp.dot(left, right, preferred_element_type=F32)
            for c in range(D // 128):
                at = c * USE * CB + u * CB
                out_ref[holder, at : at + CB, :] = total[:, c * 128 : (c + 1) * 128].astype(BF16)

        for split in (1, 2, 3):

            @pl.when(first == split)
            def _(split=split):
                emit(0, range(split))
                emit(1, range(split, 4))

        rest = parts_ref[pl.ds(holder * 2, 2), :]
        terms = []
        for _ in range(3):
            piece = rest.astype(BF16).astype(F32)
            terms.append(piece)
            rest = rest - piece
        terms.append(jnp.zeros((10, CB), F32))
        out_ref[holder, ROWS_X:, :] = jnp.concatenate(terms, axis=0).astype(BF16)


def final_pass(dist, kernel, weights, rows, got, same, target):
    return pl.pallas_call(
        final_kernel,
        grid_spec=pltpu.PrefetchScalarGridSpec(
            num_scalar_prefetch=1,
            grid=(NBD + NR,),
            in_specs=[HELD] * 6,
            out_specs=HELD,
            scratch_shapes=[
                pltpu.VMEM((ND, CB), F32),
                pltpu.VMEM((ND, CB), F32),
                pltpu.VMEM((NBD * MAXC, CB, RB), BF16),
                pltpu.SMEM((NBD * MAXC,), jnp.int32),
                pltpu.SMEM((ND,), jnp.int32),
            ],
        ),
        out_shape=pltpu.VMEM((NR, ROWS_P, 128), BF16),
        compiler_params=LIMIT,
        name="final_pass",
    )(dist, kernel, weights, rows, got, same, target)


def merge_kernel(
    wanted_ref, got_ref, target_ref, out_ref, load_ref, held, from_ref, into_ref, start_ref, out_sem
):
    chunks = D // 128

    def put(s):
        lanes = pl.ds(pl.multiple_of(s * 128, 128), 128)
        return pltpu.make_async_copy(held.at[s], out_ref.at[:, :, lanes], out_sem.at[s])

    for j in range(CBD + 2):
        start_ref[j] = 0

    @pl.loop(0, ND)
    def _(i):
        j = wanted_ref[i]
        start_ref[j + 1] = start_ref[j + 1] + 1

    @pl.loop(0, CBD)
    def _(j):
        begin = start_ref[j]
        count = start_ref[j + 1]
        start_ref[j + 1] = begin + count

        @pl.when(count == 0)
        def _():
            for s in range(chunks):
                held[s, j] = jnp.zeros((CB, 128), F32)

    @pl.loop(0, ND)
    def _(i):
        j = wanted_ref[i]
        at = start_ref[j]
        start_ref[j] = at + 1
        from_ref[at] = i
        into_ref[at] = j

    @pl.loop(0, chunks)
    def _(s):
        def add(group, carry):
            total, last = carry
            for m in range(4):
                i = from_ref[group * 4 + m]
                j = into_ref[group * 4 + m]
                at = pl.multiple_of(s * (USE * CB) + (i & 1) * CB, CB)
                part = got_ref[i >> 1, pl.ds(at, CB), :].astype(F32)
                total = part + jnp.where(j == last, total, 0.0)
                held[s, j] = total
                last = j
            return total, last

        lax.fori_loop(0, ND // 4, add, (jnp.zeros((CB, 128), F32), jnp.int32(-1)))
        put(s).start()

    load_ref[...] = jnp.zeros_like(load_ref)
    for r in range(NR):
        terms = got_ref[r, ROWS_X:, :].astype(F32)
        for u in range(USE):
            mass = terms[u : u + 1] + terms[u + 2 : u + 3] + terms[u + 4 : u + 5]
            load_ref[pl.ds(wanted_ref[r * USE + u], 1), :] += mass
    load_ref[...] = load_ref[...] / target_ref[:1]

    @pl.loop(0, chunks)
    def _(s):
        put(s).wait()


def merge(wanted, got, target):
    chunks = D // 128
    return pl.pallas_call(
        merge_kernel,
        in_specs=[pl.BlockSpec(memory_space=pltpu.SMEM), HELD, HELD],
        out_specs=[pl.BlockSpec(memory_space=pl.ANY), HELD],
        scratch_shapes=[
            pltpu.VMEM((chunks, CBD, CB, 128), F32),
            pltpu.SMEM((ND,), jnp.int32),
            pltpu.SMEM((ND,), jnp.int32),
            pltpu.SMEM((CBD + 2,), jnp.int32),
            pltpu.SemaphoreType.DMA((chunks,)),
        ],
        out_shape=[
            jax.ShapeDtypeStruct((CBD, CB, D), F32),
            jax.ShapeDtypeStruct((CBD, CB), F32),
        ],
        compiler_params=LIMIT,
        name="merge",
    )(wanted, got, target)


def exchange(values):
    return lax.all_to_all(values, "rows", split_axis=0, concat_axis=0, tiled=True)


def body(groups, centroids, row_weight, block_ids, block_counts):
    weight_rows = row_weight.reshape(NBD * RB // CB, CB)
    table, dist, unit = make_table(block_ids, weight_rows, centroids.reshape(CBD, CB, D))
    tables = lax.all_to_all(
        table.reshape(DEVICES, 1, CB), ("rows", "cents"), split_axis=0, concat_axis=0, tiled=True
    ).reshape(NR, NC, CB)
    picked, wanted, same, target = pick_lists(
        tables, table, unit
    )
    groups = groups.reshape(NBD, RB, D)
    lists = exchange(picked.reshape(NR, USE * CB, D)).reshape(ND, CB, D)

    kernel, parts, rows, weights = first_pass(dist, block_counts, groups, weight_rows, lists)
    got = exchange(parts)
    for _ in range(ITERS - 1):
        got = exchange(turn(dist, kernel, weights, got, same, target))
    sums = final_pass(dist, kernel, weights, rows, got, same, target)
    totals, load = merge(wanted, exchange(sums), target)
    return totals.reshape(-1, D), load.reshape(-1)


def solution(mesh):
    placed = (
        P(("rows", "cents"), None),
        P(("rows", "cents"), None),
        P(("rows", "cents")),
        P(("rows", "cents"), None),
        P(("rows", "cents")),
    )
    return jax.shard_map(
        body,
        mesh=mesh,
        in_specs=placed,
        out_specs=(P(("rows", "cents"), None), P(("rows", "cents"))),
        check_vma=False,
    )
```

```python
import jax
import jax.numpy as jnp
from jax import lax
from jax.experimental import pallas as pl
from jax.experimental.pallas import tpu as pltpu
from jax.sharding import PartitionSpec as P

D = 1024
RB = 256
CB = 128
MAXC = 8
USE = 2
ITERS = 3
NBD = 8
CBD = 16
NR = 16
NC = 8
ND = NR * USE
DEVICES = NR * NC
K_TOTAL = DEVICES * CBD * CB
ROWS_X = USE * CB * (D // 128)
ROWS_P = ROWS_X + 16
EARLY = NBD // 2
HOLDER_BITS = (CBD * NC).bit_length() - 1

BETA = 32.0
EPSILON = 1e-06
PRIOR = 0.25
F32 = jnp.float32
BF16 = jnp.bfloat16
HELD = pl.BlockSpec(memory_space=pltpu.VMEM)
LIMIT = pltpu.CompilerParams(vmem_limit_bytes=20 << 20)


def unit_rows(values):
    widened = values.astype(F32)
    mean = jnp.sum(widened * widened, axis=-1, keepdims=True) * (1.0 / D)
    return (widened * lax.rsqrt(mean + EPSILON)).astype(BF16)


def table_kernel(
    ids_ref, weight_ref, lists_ref, table_ref, dist_ref, unit_ref, low_ref, high_ref, raw, sem
):
    def load(n):
        return pltpu.make_async_copy(lists_ref.at[n], raw.at[n], sem.at[n])

    for n in range(CBD):
        load(n).start()
    for o in range(NR):
        low_ref[o] = -1
        high_ref[o] = -1
    part = MAXC // 2

    @pl.loop(0, CBD)
    def _(n):
        load(n).wait()
        for m in range(part):
            b = n >> 1
            k = (n & 1) * part + m
            number = ids_ref[b, k]
            holder = number >> HOLDER_BITS
            local = number & (CBD - 1)
            seen = low_ref[holder]
            low = jnp.where(seen < 0, local, seen)
            low_ref[holder] = low
            rank = jnp.where(local != low, 1, 0)
            high_ref[holder] = jnp.where(rank == 1, local, high_ref[holder])
            dist_ref[n * part + m] = holder * USE + rank
        unit_ref[n] = unit_rows(raw[n])

    weight = jnp.sum(jnp.sum(weight_ref[...], axis=0, keepdims=True), axis=1, keepdims=True)
    lane = lax.broadcasted_iota(jnp.int32, (1, CB), 1)
    numbers = jnp.zeros((1, CB), jnp.int32)
    for o in range(NR):
        low = low_ref[o]
        high = high_ref[o]
        is_low = (lane == USE * o) | (lane == ND + USE * o + 1)
        is_high = (lane == USE * o + 1) | (lane == ND + USE * o)
        numbers = jnp.where(is_low, low, jnp.where(is_high, high, numbers))
    row = jnp.where(lane < 2 * ND, numbers.astype(F32), jnp.broadcast_to(weight, (1, CB)))
    table_ref[...] = jnp.broadcast_to(row, (DEVICES, CB))


def make_table(block_ids, weight_rows, centroids):
    smem = pl.BlockSpec(memory_space=pltpu.SMEM)
    return pl.pallas_call(
        table_kernel,
        in_specs=[smem, HELD, pl.BlockSpec(memory_space=pl.ANY)],
        out_specs=[HELD, smem, HELD],
        out_shape=[
            pltpu.VMEM((DEVICES, CB), F32),
            jax.ShapeDtypeStruct((NBD * MAXC,), jnp.int32),
            pltpu.VMEM((CBD, CB, D), BF16),
        ],
        scratch_shapes=[
            pltpu.SMEM((NR,), jnp.int32),
            pltpu.SMEM((NR,), jnp.int32),
            pltpu.VMEM((CBD, CB, D), BF16),
            pltpu.SemaphoreType.DMA((CBD,)),
        ],
        compiler_params=pltpu.CompilerParams(vmem_limit_bytes=57 << 20),
        name="make_table",
    )(block_ids, weight_rows, centroids)


def prepare(rows, mine, tables_ref, same_ref, target_ref):
    filler = jnp.zeros((CB - NR - 1, CB), F32)
    turned = jnp.transpose(jnp.concatenate([rows, mine, filler], axis=0))
    here = turned[:ND, NR : NR + 1]
    other = turned[ND : 2 * ND, NR : NR + 1]
    for r in range(NR):
        theirs = turned[:ND, r : r + 1]
        same_ref[0, r] = jnp.broadcast_to(jnp.where(theirs == here, 1.0, 0.0), (ND, CB))
        same_ref[1, r] = jnp.broadcast_to(jnp.where(theirs == other, 1.0, 0.0), (ND, CB))
    total = jnp.sum(jnp.sum(tables_ref[...], axis=0), axis=0, keepdims=True)
    lane = lax.broadcasted_iota(jnp.int32, (1, CB), 1)
    mass = jnp.sum(jnp.where(lane == CB - 1, total, 0.0), axis=1, keepdims=True)
    target_ref[...] = jnp.broadcast_to(mass * (1.0 / K_TOTAL), (8, CB))


def pick_kernel(
    tables_ref,
    table_ref,
    lists_ref,
    out_ref,
    wanted_ref,
    same_ref,
    target_ref,
    numbers,
    scalars,
    move_sem,
):
    me = lax.axis_index("rows")
    side = lax.axis_index("cents")

    rows = jnp.concatenate([tables_ref[r, pl.ds(side, 1), :] for r in range(NR)], axis=0)
    numbers[...] = rows.astype(jnp.int32)
    move = pltpu.make_async_copy(numbers, scalars, move_sem)
    move.start()
    prepare(rows, table_ref[:1], tables_ref, same_ref, target_ref)

    move.wait()

    @pl.loop(0, NR)
    def _(r):
        for u in range(USE):
            j = scalars[r, me * USE + u]
            wanted_ref[r * USE + u] = j
            out_ref[r * USE + u] = lists_ref[j]


def pick_lists(tables, table, unit):
    return pl.pallas_call(
        pick_kernel,
        in_specs=[HELD, HELD, HELD],
        out_specs=[HELD, pl.BlockSpec(memory_space=pltpu.SMEM), HELD, HELD],
        out_shape=[
            pltpu.VMEM((ND, CB, D), BF16),
            jax.ShapeDtypeStruct((ND,), jnp.int32),
            pltpu.VMEM((2, NR, ND, CB), F32),
            pltpu.VMEM((8, CB), F32),
        ],
        scratch_shapes=[
            pltpu.VMEM((NR, CB), jnp.int32),
            pltpu.SMEM((NR, CB), jnp.int32),
            pltpu.SemaphoreType.DMA,
        ],
        compiler_params=LIMIT,
        name="pick_lists",
    )(tables, table, unit)


def column_pass(kernel_ref, row_scale, dist_ref, b, parts_ref):
    for k in range(MAXC):
        part = jnp.sum(kernel_ref[b, k] * row_scale, axis=0, keepdims=True)
        d = dist_ref[b * MAXC + k]
        parts_ref[pl.ds(d, 1), :] += part


def spread(parts_ref, out_ref):
    parts = parts_ref[...]
    for r in range(NR):
        out_ref[r] = parts


STEP = 4


def scores_kernel(dist_ref, count_ref, *refs):
    groups_ref, mass_ref, lists_ref, kernel_ref, out_ref, rows_ref, weight_ref, parts_ref = refs
    step = pl.program_id(0)

    @pl.when(step == 0)
    def _():
        parts_ref[...] = jnp.zeros_like(parts_ref)

    for n in range(STEP):
        b = step * STEP + n
        count = count_ref[b]
        rows = unit_rows(groups_ref[b])
        rows_ref[b] = rows
        halves = []
        for h in range(RB // CB):
            flat = jnp.broadcast_to(mass_ref[pl.ds(b * (RB // CB) + h, 1), :], (CB, CB))
            halves.append(jnp.transpose(flat))
        weight = jnp.concatenate(halves, axis=0)
        weight_ref[b] = weight
        total = jnp.zeros((RB, CB), F32)
        for k in range(0, MAXC, 2):
            named = [dist_ref[b * MAXC + k + m] for m in range(2)]
            pair = jnp.concatenate([lists_ref[d] for d in named], axis=0)
            scores = lax.dot_general(
                rows, pair, (((1,), (1,)), ((), ())), preferred_element_type=F32
            )
            grown = jnp.exp(scores * (BETA / D))
            for m in range(2):
                live = jnp.where(k + m < count, grown[:, m * CB : (m + 1) * CB], 0.0)
                kernel_ref[b, k + m] = live
                total = total + live
        row_scale = weight / jnp.sum(total, axis=1, keepdims=True)
        column_pass(kernel_ref, row_scale, dist_ref, b, parts_ref)

    @pl.when(step == NBD // STEP - 1)
    def _():
        spread(parts_ref, out_ref)


def first_pass(dist, counts, groups, weight_rows, lists):
    return pl.pallas_call(
        scores_kernel,
        grid_spec=pltpu.PrefetchScalarGridSpec(
            num_scalar_prefetch=2,
            grid=(NBD // STEP,),
            in_specs=[HELD] * 3,
            out_specs=[HELD] * 4,
            scratch_shapes=[pltpu.VMEM((ND, CB), F32)],
        ),
        out_shape=[
            pltpu.VMEM((NBD, MAXC, RB, CB), F32),
            jax.ShapeDtypeStruct((NR, ND, CB), F32),
            pltpu.VMEM((NBD, RB, D), BF16),
            pltpu.VMEM((NBD, RB, CB), F32),
        ],
        compiler_params=LIMIT,
        name="scores",
    )(dist, counts, groups, weight_rows, lists)


def new_scales(got_ref, same_ref, target_ref, scales_ref):
    straight = jnp.zeros((ND, CB), F32)
    crossed = jnp.zeros((ND, CB), F32)
    for r in range(NR):
        got = got_ref[r]
        straight = straight + same_ref[0, r] * got
        crossed = crossed + same_ref[1, r] * got
    even = lax.broadcasted_iota(jnp.int32, (ND, CB), 0) % 2 == 0
    swapped = jnp.where(even, jnp.roll(crossed, -1, axis=0), jnp.roll(crossed, 1, axis=0))
    column = straight + swapped
    target = target_ref[:1]
    scales_ref[...] = target / (column + PRIOR * target)


def row_pass(kernel_ref, weight_ref, scales_ref, dist_ref, b):
    total = jnp.zeros((RB, CB), F32)
    for k in range(MAXC):
        d = dist_ref[b * MAXC + k]
        total = total + kernel_ref[b, k] * scales_ref[pl.ds(d, 1), :]
    return weight_ref[b] / jnp.sum(total, axis=1, keepdims=True)


def turn_kernel(
    dist_ref, kernel_ref, weight_ref, got_ref, same_ref, target_ref, out_ref, scales_ref, parts_ref
):
    step = pl.program_id(0)

    @pl.when(step == 0)
    def _():
        new_scales(got_ref, same_ref, target_ref, scales_ref)
        parts_ref[...] = jnp.zeros_like(parts_ref)

    for n in range(STEP):
        b = step * STEP + n
        row_scale = row_pass(kernel_ref, weight_ref, scales_ref, dist_ref, b)
        column_pass(kernel_ref, row_scale, dist_ref, b, parts_ref)

    @pl.when(step == NBD // STEP - 1)
    def _():
        spread(parts_ref, out_ref)


def turn(dist, kernel, weights, got, same, target):
    return pl.pallas_call(
        turn_kernel,
        grid_spec=pltpu.PrefetchScalarGridSpec(
            num_scalar_prefetch=1,
            grid=(NBD // STEP,),
            in_specs=[HELD] * 5,
            out_specs=HELD,
            scratch_shapes=[pltpu.VMEM((ND, CB), F32), pltpu.VMEM((ND, CB), F32)],
        ),
        out_shape=jax.ShapeDtypeStruct((NR, ND, CB), F32),
        compiler_params=LIMIT,
        name="turn",
    )(dist, kernel, weights, got, same, target)


def final_kernel(
    dist_ref,
    kernel_ref,
    weight_ref,
    rows_ref,
    got_ref,
    same_ref,
    target_ref,
    out_ref,
    scales_ref,
    parts_ref,
    plan_keep,
    order_ref,
    seen_ref,
):
    step = pl.program_id(0)

    @pl.when(step == 0)
    def _():
        new_scales(got_ref, same_ref, target_ref, scales_ref)
        parts_ref[...] = jnp.zeros_like(parts_ref)

        for d in range(ND):
            seen_ref[d] = 0

    @pl.when(step < EARLY)
    def _():
        for half in range(NBD // EARLY):
            b = step * (NBD // EARLY) + half
            row_scale = row_pass(kernel_ref, weight_ref, scales_ref, dist_ref, b)
            for k in range(MAXC):
                d = dist_ref[b * MAXC + k]
                plan = row_scale * kernel_ref[b, k] * scales_ref[pl.ds(d, 1), :]
                parts_ref[pl.ds(d, 1), :] += jnp.sum(plan, axis=0, keepdims=True)
                plan_keep[b * MAXC + k] = jnp.transpose(plan.astype(BF16))
                n = seen_ref[d]
                seen_ref[d] = n + 1
                order_ref[(d >> 1) * 4 + jnp.where(d & 1 == 0, n, 3 - n)] = b * MAXC + k

    @pl.when(step >= EARLY)
    def _():
        holder = step - EARLY
        slots = [order_ref[holder * 4 + n] for n in range(4)]
        plans = [plan_keep[p] for p in slots]
        first = seen_ref[holder * 2]

        def emit(u, chosen):
            left = jnp.concatenate([plans[n] for n in chosen], axis=1)
            right = jnp.concatenate([rows_ref[slots[n] >> 3] for n in chosen], axis=0)
            total = jnp.dot(left, right, preferred_element_type=F32)
            for c in range(D // 128):
                at = c * USE * CB + u * CB
                out_ref[holder, at : at + CB, :] = total[:, c * 128 : (c + 1) * 128].astype(BF16)

        for split in (1, 2, 3):

            @pl.when(first == split)
            def _(split=split):
                emit(0, range(split))
                emit(1, range(split, 4))

        rest = parts_ref[pl.ds(holder * 2, 2), :]
        terms = []
        for _ in range(3):
            piece = rest.astype(BF16).astype(F32)
            terms.append(piece)
            rest = rest - piece
        terms.append(jnp.zeros((10, CB), F32))
        out_ref[holder, ROWS_X:, :] = jnp.concatenate(terms, axis=0).astype(BF16)


def final_pass(dist, kernel, weights, rows, got, same, target):
    return pl.pallas_call(
        final_kernel,
        grid_spec=pltpu.PrefetchScalarGridSpec(
            num_scalar_prefetch=1,
            grid=(EARLY + NR,),
            in_specs=[HELD] * 6,
            out_specs=HELD,
            scratch_shapes=[
                pltpu.VMEM((ND, CB), F32),
                pltpu.VMEM((ND, CB), F32),
                pltpu.VMEM((NBD * MAXC, CB, RB), BF16),
                pltpu.SMEM((NBD * MAXC,), jnp.int32),
                pltpu.SMEM((ND,), jnp.int32),
            ],
        ),
        out_shape=pltpu.VMEM((NR, ROWS_P, 128), BF16),
        compiler_params=LIMIT,
        name="final_pass",
    )(dist, kernel, weights, rows, got, same, target)


def merge_kernel(
    wanted_ref, got_ref, target_ref, out_ref, load_ref, held, from_ref, into_ref, start_ref, out_sem
):
    chunks = D // 128

    def put(s):
        lanes = pl.ds(pl.multiple_of(s * 128, 128), 128)
        return pltpu.make_async_copy(held.at[s], out_ref.at[:, :, lanes], out_sem.at[s])

    for j in range(CBD + 2):
        start_ref[j] = 0

    @pl.loop(0, ND)
    def _(i):
        j = wanted_ref[i]
        start_ref[j + 1] = start_ref[j + 1] + 1

    @pl.loop(0, CBD)
    def _(j):
        begin = start_ref[j]
        count = start_ref[j + 1]
        start_ref[j + 1] = begin + count

        @pl.when(count == 0)
        def _():
            for s in range(chunks):
                held[s, j] = jnp.zeros((CB, 128), F32)

    @pl.loop(0, ND)
    def _(i):
        j = wanted_ref[i]
        at = start_ref[j]
        start_ref[j] = at + 1
        from_ref[at] = i
        into_ref[at] = j

    @pl.loop(0, chunks)
    def _(s):
        def add(group, carry):
            total, last = carry
            for m in range(4):
                i = from_ref[group * 4 + m]
                j = into_ref[group * 4 + m]
                at = pl.multiple_of(s * (USE * CB) + (i & 1) * CB, CB)
                part = got_ref[i >> 1, pl.ds(at, CB), :].astype(F32)
                total = part + jnp.where(j == last, total, 0.0)
                held[s, j] = total
                last = j
            return total, last

        lax.fori_loop(0, ND // 4, add, (jnp.zeros((CB, 128), F32), jnp.int32(-1)))
        put(s).start()

    load_ref[...] = jnp.zeros_like(load_ref)
    for r in range(NR):
        terms = got_ref[r, ROWS_X:, :].astype(F32)
        for u in range(USE):
            mass = terms[u : u + 1] + terms[u + 2 : u + 3] + terms[u + 4 : u + 5]
            load_ref[pl.ds(wanted_ref[r * USE + u], 1), :] += mass
    load_ref[...] = load_ref[...] / target_ref[:1]

    @pl.loop(0, chunks)
    def _(s):
        put(s).wait()


def merge(wanted, got, target):
    chunks = D // 128
    return pl.pallas_call(
        merge_kernel,
        in_specs=[pl.BlockSpec(memory_space=pltpu.SMEM), HELD, HELD],
        out_specs=[pl.BlockSpec(memory_space=pl.ANY), HELD],
        scratch_shapes=[
            pltpu.VMEM((chunks, CBD, CB, 128), F32),
            pltpu.SMEM((ND,), jnp.int32),
            pltpu.SMEM((ND,), jnp.int32),
            pltpu.SMEM((CBD + 2,), jnp.int32),
            pltpu.SemaphoreType.DMA((chunks,)),
        ],
        out_shape=[
            jax.ShapeDtypeStruct((CBD, CB, D), F32),
            jax.ShapeDtypeStruct((CBD, CB), F32),
        ],
        compiler_params=LIMIT,
        name="merge",
    )(wanted, got, target)


def exchange(values):
    return lax.all_to_all(values, "rows", split_axis=0, concat_axis=0, tiled=True)


def body(groups, centroids, row_weight, block_ids, block_counts):
    weight_rows = row_weight.reshape(NBD * RB // CB, CB)
    table, dist, unit = make_table(block_ids, weight_rows, centroids.reshape(CBD, CB, D))
    tables = lax.all_to_all(
        table.reshape(DEVICES, 1, CB), ("rows", "cents"), split_axis=0, concat_axis=0, tiled=True
    ).reshape(NR, NC, CB)
    picked, wanted, same, target = pick_lists(
        tables, table, unit
    )
    groups = groups.reshape(NBD, RB, D)
    lists = exchange(picked.reshape(NR, USE * CB, D)).reshape(ND, CB, D)

    kernel, parts, rows, weights = first_pass(dist, block_counts, groups, weight_rows, lists)
    got = exchange(parts)
    for _ in range(ITERS - 1):
        got = exchange(turn(dist, kernel, weights, got, same, target))
    sums = final_pass(dist, kernel, weights, rows, got, same, target)
    totals, load = merge(wanted, exchange(sums), target)
    return totals.reshape(-1, D), load.reshape(-1)


def solution(mesh):
    placed = (
        P(("rows", "cents"), None),
        P(("rows", "cents"), None),
        P(("rows", "cents")),
        P(("rows", "cents"), None),
        P(("rows", "cents")),
    )
    return jax.shard_map(
        body,
        mesh=mesh,
        in_specs=placed,
        out_specs=(P(("rows", "cents"), None), P(("rows", "cents"))),
        check_vma=False,
    )
```
